128 devices in a mesh: row: 8 (over z, core), col: 16 (over x, y).
Axes of the slice: x: 4, y: 4, z: 4, core: 2. Of those that a mesh axis runs over, the one named last changes fastest.
Arguments:
- tokens: bfloat16 [2048, 4096], P('row', 'col'), may hold values from -6 to 6
- lengths: int32 [64], P('col'), may hold values from 1 to 64, as said below
- adapter_ids: int32 [64], P('col'), may hold values from 0 to 255, as said below
- adapter_place: int32 [256], replicated, may hold values from 0 to 255, as said below
- attention_qkv_weight: bfloat16 [2048, 6144], P('col', 'row'), may hold values from -0.125 to 0.125
- attention_out_weight: bfloat16 [2048, 2048], P('col', 'row'), may hold values from -0.125 to 0.125
- widen_weight: bfloat16 [2048, 8192], P('col', 'row'), may hold values from -0.125 to 0.125
- contract_weight: bfloat16 [2048, 8192], P('col', 'row'), may hold values from -0.0625 to 0.0625
- first_gain: float32 [2048], P('row'), may hold values from 0.5 to 1.5
- first_shift: float32 [2048], replicated, may hold values from -3 to 3
- second_gain: float32 [2048], replicated, may hold values from 0.5 to 1.5
- second_shift: float32 [2048], replicated, may hold values from -3 to 3
- attend_shrink: bfloat16 [256, 192, 2048], P('col', None, 'row'), may hold values from -0.125 to 0.125
- attend_expand: bfloat16 [256, 3, 64, 2048], P('col', None, None, 'row'), may hold values from -0.75 to 0.75
- output_shrink: bfloat16 [256, 64, 2048], P('col', None, 'row'), may hold values from -0.125 to 0.125
- output_expand: bfloat16 [256, 64, 2048], P('col', None, 'row'), may hold values from -0.75 to 0.75
- upward_shrink: bfloat16 [256, 64, 2048], P('col', None, 'row'), may hold values from -0.125 to 0.125
- upward_expand: bfloat16 [256, 64, 8192], P('col', None, 'row'), may hold values from -0.75 to 0.75
- downward_shrink: bfloat16 [256, 64, 8192], P('col', None, 'row'), may hold values from -0.0625 to 0.0625
- downward_expand: bfloat16 [256, 64, 2048], P('col', None, 'row'), may hold values from -0.75 to 0.75
Outputs:
- layer_out: bfloat16 [2048, 4096], P(None, 'col')
The draws below stay inside these ranges and needn't reach their ends.
Inputs may be any that keep to these rules, and one draw needn't show every extreme that they name: `lengths`: each aligned block of 4 requests holds a prompt of exactly 64 tokens. `adapter_ids`: in each aligned block of 4 requests, at most 2 name adapters whose store positions lie in one aligned block of 16 positions, and exactly 2 do for some such block. `adapter_place`: A permutation.
All inputs are finite; a program needn't handle non-finite values.
Results may differ from the reference program's by a relative error of at most 0.024.
Values may be sent and summed in bfloat16 or wider, within the bound.
A program may use at most 128 MiB of HBM per device.

```python
import math
import jax
import jax.numpy as jnp
from jax import lax

D = 2048
H = 16
HD = 128
FF = 8192
R = 64
ADP_COL = 16
SLOT = 64
REQ_COL = 4
ADAPTERS = 256
REQUESTS = 64
TOKENS = 4096


def adapter_table(key):
    return jax.random.permutation(jax.random.fold_in(key, 11), ADAPTERS).astype(jnp.int32)


def draw_adapter_place(key, part):
    return adapter_table(key)


def draw_adapter_ids(key, part):
    place = adapter_table(key)
    inverse = jnp.argsort(place).astype(jnp.int32)
    column_count = REQUESTS // REQ_COL
    half = column_count // 2
    forced = jax.random.randint(jax.random.fold_in(key, 29), (), 0, column_count).astype(jnp.int32)

    def column(column_key, index):
        key_one, key_two, key_three, key_four = jax.random.split(column_key, 4)
        order = jax.random.permutation(key_one, column_count).astype(jnp.int32)
        target = (index + half) % column_count
        found = jnp.argmax(order == target).astype(jnp.int32)
        rolled = jnp.roll(order, -found)
        order = jnp.where(index == forced, rolled, order).astype(jnp.int32)
        others = jnp.concatenate([order[1:], order[1:]])
        others = others[jax.random.permutation(key_two, others.shape[0])]
        owners = jnp.concatenate([jnp.stack([order[0], order[0]]), others])[:REQ_COL]
        owners = owners[jax.random.permutation(key_three, REQ_COL)]
        local = jax.random.randint(key_four, (REQ_COL,), 0, ADP_COL).astype(jnp.int32)
        return inverse[owners * ADP_COL + local]
    column_keys = jax.random.split(jax.random.fold_in(key, 23), column_count)
    indices = jnp.arange(column_count, dtype=jnp.int32)
    return jax.vmap(column)(column_keys, indices).reshape(REQUESTS).astype(jnp.int32)


def draw_lengths(key, part):
    key_one, key_two = jax.random.split(jax.random.fold_in(key, 37))
    base = jax.random.randint(key_one, (REQUESTS,), 1, SLOT + 1).astype(jnp.int32)
    column_count = REQUESTS // REQ_COL
    chosen = jax.random.randint(key_two, (column_count,), 0, REQ_COL)
    longest = (jnp.arange(REQ_COL)[None, :] == chosen[:, None]).reshape(REQUESTS)
    return jnp.where(longest, SLOT, base).astype(jnp.int32)


def block_levels(own_key, extent, pieces, smallest, largest):
    def one(dim, shards_of):
        draws = jax.random.uniform(jax.random.fold_in(jax.random.fold_in(own_key, 6), dim), (shards_of,), jnp.float32, smallest / len(pieces), largest / len(pieces))
        return jnp.repeat(jnp.exp(draws), extent[dim] // shards_of).reshape((-1,) + (1,) * (len(extent) - dim - 1))

    loudness = one(*pieces[0])
    for cut in pieces[1:]:
        loudness = loudness * one(*cut)
    return loudness


def normal_values(own_key, dims, spread, limit, cuts=(), kind=jnp.bfloat16):
    factor_of = block_levels(own_key, dims, cuts, -0.22, 0.18) if cuts else 1.0
    drawn = jax.random.normal(own_key, dims, jnp.float32) * spread * factor_of
    return jnp.minimum(jnp.maximum(drawn, -limit), limit).astype(kind)


def setup_inputs(seed: int = 0) -> dict:
    key_list = jax.random.split(jax.random.key(seed), 21)
    return {
        "tokens": normal_values(key_list[0], (D, TOKENS), 1.0, 6.0, ((0, 8), (1, 16))),
        "lengths": draw_lengths(jax.random.fold_in(key_list[20], 71), 0),
        "adapter_ids": draw_adapter_ids(jax.random.fold_in(key_list[20], 71), 0),
        "adapter_place": draw_adapter_place(jax.random.fold_in(key_list[20], 71), 0),
        "attention_qkv_weight": normal_values(key_list[4], (D, 3 * D), D ** -0.5, 0.125, ((0, 16), (1, 8))),
        "attention_out_weight": normal_values(key_list[5], (D, D), D ** -0.5, 0.125, ((0, 16), (1, 8))),
        "widen_weight": normal_values(key_list[6], (D, FF), D ** -0.5, 0.125, ((0, 16), (1, 8))),
        "contract_weight": normal_values(key_list[7], (D, FF), FF ** -0.5, 0.0625, ((0, 16), (1, 8))),
        "first_gain": jnp.clip(1.0 + 0.1 * jax.random.normal(key_list[8], (D,), jnp.float32), 0.5, 1.5),
        "first_shift": normal_values(key_list[9], (D,), 0.3, 3.0, (), jnp.float32),
        "second_gain": jnp.clip(1.0 + 0.1 * jax.random.normal(key_list[10], (D,), jnp.float32), 0.5, 1.5),
        "second_shift": normal_values(key_list[11], (D,), 0.3, 3.0, (), jnp.float32),
        "attend_shrink": normal_values(key_list[12], (ADAPTERS, 3 * R, D), D ** -0.5, 0.125, ((0, 16), (2, 8))),
        "attend_expand": normal_values(key_list[13], (ADAPTERS, 3, R, D), R ** -0.5, 0.75, ((0, 16), (3, 8))),
        "output_shrink": normal_values(key_list[14], (ADAPTERS, R, D), D ** -0.5, 0.125, ((0, 16), (2, 8))),
        "output_expand": normal_values(key_list[15], (ADAPTERS, R, D), R ** -0.5, 0.75, ((0, 16), (2, 8))),
        "upward_shrink": normal_values(key_list[16], (ADAPTERS, R, D), D ** -0.5, 0.125, ((0, 16), (2, 8))),
        "upward_expand": normal_values(key_list[17], (ADAPTERS, R, FF), R ** -0.5, 0.75, ((0, 16), (2, 8))),
        "downward_shrink": normal_values(key_list[18], (ADAPTERS, R, FF), FF ** -0.5, 0.0625, ((0, 16), (2, 8))),
        "downward_expand": normal_values(key_list[19], (ADAPTERS, R, D), R ** -0.5, 0.75, ((0, 16), (2, 8))),
    }


eps = 1e-12
lowrank_scale = 0.5

def shrink_all(store, position, inputs):
    blocks = jnp.moveaxis(inputs.reshape(inputs.shape[0], REQUESTS, SLOT), 1, 0)

    def single(item):
        index, block = item
        matrix = lax.dynamic_index_in_dim(store, index, 0, keepdims=False)
        return jnp.dot(matrix, block, preferred_element_type=jnp.float32).astype(jnp.bfloat16)
    return lax.map(single, (position, blocks))

def expand_all(store, position, reduced):

    def single(item):
        index, block = item
        matrix = lax.dynamic_index_in_dim(store, index, 0, keepdims=False)
        return jnp.dot(matrix.T, block, preferred_element_type=jnp.float32).astype(jnp.bfloat16)
    result = lax.map(single, (position, reduced))
    return jnp.moveaxis(result, 0, 1).reshape(result.shape[1], TOKENS)

def expanded_combined(store, position, reduced):

    def single(item):
        index, block = item
        matrix = lax.dynamic_index_in_dim(store, index, 0, keepdims=False).astype(jnp.float32)
        grouped = block.reshape(3, R, SLOT).astype(jnp.float32)
        part = jnp.einsum('jko,jks->jos', matrix, grouped)
        part = part.reshape(3, H, HD, SLOT).transpose(1, 0, 2, 3).reshape(3 * D, SLOT)
        return part.astype(jnp.bfloat16)
    result = lax.map(single, (position, reduced))
    return jnp.moveaxis(result, 0, 1).reshape(3 * D, TOKENS)

def normalize(values, gain, shift):
    mean = lax.optimization_barrier(jnp.mean(values, axis=0))
    square_mean = lax.optimization_barrier(jnp.mean(values * values, axis=0))
    factor = lax.rsqrt(square_mean - mean * mean + eps)
    return (values - mean) * factor * gain[:, None] + shift[:, None]

def reference(tokens, lengths, adapter_ids, adapter_place, attention_qkv_weight, attention_out_weight, widen_weight, contract_weight, first_gain, first_shift, second_gain, second_shift, attend_shrink, attend_expand, output_shrink, output_expand, upward_shrink, upward_expand, downward_shrink, downward_expand):
    position = adapter_place[adapter_ids].astype(jnp.int32)
    lowrank_update = expanded_combined(attend_expand, position, shrink_all(attend_shrink, position, tokens))
    combined_parts = jnp.dot(attention_qkv_weight.T, tokens, preferred_element_type=jnp.float32) + lowrank_scale * lowrank_update.astype(jnp.float32)
    combined_parts = combined_parts.astype(jnp.bfloat16).reshape(H, 3, HD, REQUESTS, SLOT)
    query = combined_parts[:, 0].astype(jnp.float32)
    keys = combined_parts[:, 1].astype(jnp.float32)
    values = combined_parts[:, 2].astype(jnp.float32)
    scores = jnp.einsum('hdrq,hdrk->hrqk', query, keys) / math.sqrt(HD)
    valid = jnp.arange(SLOT, dtype=jnp.int32)[None, :] < lengths[:, None]
    weights = jnp.where(valid[None, :, None, :], jnp.exp(scores), 0.0)
    probs = (weights / lax.optimization_barrier(jnp.sum(weights, axis=3, keepdims=True))).astype(jnp.bfloat16)
    attended_context = jnp.einsum('hdrk,hrqk->hdrq', values, probs.astype(jnp.float32)).astype(jnp.bfloat16).reshape(D, TOKENS)
    lowrank_update = expand_all(output_expand, position, shrink_all(output_shrink, position, attended_context))
    first_residual_input = tokens.astype(jnp.float32) + jnp.dot(attention_out_weight.T, attended_context, preferred_element_type=jnp.float32) + lowrank_scale * lowrank_update.astype(jnp.float32)
    first_norm_output = normalize(first_residual_input, first_gain, first_shift).astype(jnp.bfloat16)
    lowrank_update = expand_all(upward_expand, position, shrink_all(upward_shrink, position, first_norm_output))
    hidden_units = jnp.dot(widen_weight.T, first_norm_output, preferred_element_type=jnp.float32) + lowrank_scale * lowrank_update.astype(jnp.float32)
    hidden_units = jax.nn.gelu(hidden_units, approximate=True).astype(jnp.bfloat16)
    lowrank_update = expand_all(downward_expand, position, shrink_all(downward_shrink, position, hidden_units))
    second_residual_input = first_norm_output.astype(jnp.float32) + jnp.dot(contract_weight, hidden_units, preferred_element_type=jnp.float32) + lowrank_scale * lowrank_update.astype(jnp.float32)
    return normalize(second_residual_input, second_gain, second_shift).astype(jnp.bfloat16)
```

```python
import functools
import math

import jax
import jax.numpy as jnp
from jax import lax
from jax.experimental import pallas as pl
from jax.experimental.pallas import tpu as pltpu
from jax.sharding import PartitionSpec as P

D = 2048
HD = 128
SLOT = 64
RANK = 64
GRP = 4
TOK = GRP * SLOT
K = 12
REQ_COL = 4

eps = 1e-12
lowrank_scale = 0.5

MESH = pl.DeviceIdType.MESH
HBM = pl.BlockSpec(memory_space=pl.ANY)
NT = (((1,), (1,)), ((), ()))
f32 = jnp.float32
bf16 = jnp.bfloat16


def dot(a, b):
    return jnp.dot(a, b, preferred_element_type=f32)


def dot_nt(a, b):
    return lax.dot_general(a, b, NT, preferred_element_type=f32)


def greet(peers):
    barrier = pltpu.get_barrier_semaphore()
    for peer in peers:
        pl.semaphore_signal(barrier, inc=1, device_id=peer, device_id_type=MESH)
    pl.semaphore_wait(barrier, len(peers))


class Sender:
    def __init__(self, send_sem, recv_sem):
        self.send_sem, self.recv_sem = send_sem, recv_sem
        self.copies = []

    def start(self, src, dst, peer):
        i = len(self.copies)
        copy = pltpu.make_async_remote_copy(
            src_ref=src,
            dst_ref=dst,
            send_sem=self.send_sem.at[i],
            recv_sem=self.recv_sem.at[i],
            device_id=peer,
            device_id_type=MESH,
        )
        copy.start()
        self.copies.append(copy)
        return copy


def row_place():
    row = lax.axis_index("row")
    col = lax.axis_index("col")
    z, core = row // 2, row % 2
    return row, col, z, core


def ring_gather(buf, row, col, z, core, sender):
    half = buf.shape[1] // 2
    up, down = (z + 1) % 4, (z + 3) % 4
    far = (z + 2) % 4

    def part(zz, h):
        return buf.at[zz * 2 + core, pl.ds(h * half, half)]

    def dev(zz):
        return (zz * 2 + core, col)

    partner = (z * 2 + 1 - core, col)
    a0 = sender.start(part(z, 0), part(z, 0), dev(up))
    b1 = sender.start(part(z, 1), part(z, 1), dev(down))
    a1 = sender.start(part(z, 1), part(z, 1), dev(up))
    b0 = sender.start(part(z, 0), part(z, 0), dev(down))
    own = sender.start(buf.at[row], buf.at[row], partner)
    rest = [own]

    def across(zz, h):
        rest.append(sender.start(part(zz, h), part(zz, h), partner))

    a0.wait_recv()
    r0 = sender.start(part(down, 0), part(down, 0), dev(up))
    across(down, 0)
    b1.wait_recv()
    r1 = sender.start(part(up, 1), part(up, 1), dev(down))
    across(up, 1)
    a1.wait_recv()
    across(down, 1)
    b0.wait_recv()
    across(up, 0)
    r0.wait_recv()
    across(far, 0)
    r1.wait_recv()
    across(far, 1)
    for copy in rest:
        copy.wait_recv()


def row_neighbours(col, z, core):
    return [
        (((z + 1) % 4) * 2 + core, col),
        (((z + 3) % 4) * 2 + core, col),
        (z * 2 + 1 - core, col),
    ]


def row_gather_kernel(in_ref, out_ref, send_sem, recv_sem):
    row, col, z, core = row_place()
    greet(row_neighbours(col, z, core))
    sender = Sender(send_sem, recv_sem)
    ring_gather(out_ref, row, col, z, core, sender)
    for copy in sender.copies:
        copy.wait_send()


def row_gather(buf, cid):
    return pl.pallas_call(
        row_gather_kernel,
        out_shape=jax.ShapeDtypeStruct(buf.shape, buf.dtype),
        in_specs=[HBM],
        out_specs=HBM,
        scratch_shapes=[pltpu.SemaphoreType.DMA((13,)), pltpu.SemaphoreType.DMA((13,))],
        input_output_aliases={0: 0},
        compiler_params=pltpu.CompilerParams(collective_id=cid, has_side_effects=True),
        name="row_gather",
    )(buf)


def stat_gather_kernel(in_ref, out_ref, send_sem, recv_sem, own_sem):
    row = lax.axis_index("row")
    col = lax.axis_index("col")
    peers = [((row + i) % 8, col) for i in range(1, 8)]
    own = pltpu.make_async_copy(in_ref, out_ref.at[row], own_sem)
    own.start()
    greet(peers)
    sender = Sender(send_sem, recv_sem)
    for peer in peers:
        sender.start(in_ref, out_ref.at[row], peer)
    own.wait()
    for copy in sender.copies:
        copy.wait()


def stat_gather(part, cid):
    return pl.pallas_call(
        stat_gather_kernel,
        out_shape=jax.ShapeDtypeStruct((8,) + part.shape, part.dtype),
        in_specs=[pl.BlockSpec(memory_space=pltpu.VMEM)],
        out_specs=pl.BlockSpec(memory_space=pltpu.VMEM),
        scratch_shapes=[
            pltpu.SemaphoreType.DMA((7,)),
            pltpu.SemaphoreType.DMA((7,)),
            pltpu.SemaphoreType.DMA,
        ],
        compiler_params=pltpu.CompilerParams(collective_id=cid, has_side_effects=True),
        name="stat_gather",
    )(part)


def torus_gather(src, dst, row, x, y, sender):
    rows = src.shape[0]
    half, quarter = rows // 2, rows // 4

    def step(p, d):
        return (p + d) % 4

    flows = []
    for first in (0, 1):
        base = first * half

        def at(a, b, first=first):
            return (a * 4 + b) if first == 0 else (b * 4 + a)

        p, q = (x, y) if first == 0 else (y, x)

        def dev(a, b, at=at):
            return (row, at(a, b))

        def blk(a, b, lo, n, at=at, base=base):
            return dst.at[at(a, b), pl.ds(base + lo, n)]

        own = src.at[pl.ds(base, half)]
        flows.append((p, q, dev, blk, own))

    state = []
    for p, q, dev, blk, own in flows:
        here = blk(p, q, 0, half)
        a = sender.start(own, here, dev(step(p, 1), q))
        b = sender.start(own, here, dev(step(p, 3), q))
        c = sender.start(own, here, dev(p, step(q, 1)))
        d = sender.start(own, here, dev(p, step(q, 3)))
        state.append([a, b, [(p, c, d)]])
    yield
    relays = []
    for (p, q, dev, blk, own), st in zip(flows, state):
        a, b, second = st
        lo, hi = step(p, 3), step(p, 1)
        a.wait_recv()
        v = blk(lo, q, 0, quarter)
        r0 = sender.start(v, v, dev(step(p, 1), q))
        v = blk(lo, q, 0, half)
        second.append(
            (lo, sender.start(v, v, dev(p, step(q, 1))), sender.start(v, v, dev(p, step(q, 3))))
        )
        b.wait_recv()
        v = blk(hi, q, quarter, quarter)
        r1 = sender.start(v, v, dev(step(p, 3), q))
        v = blk(hi, q, 0, half)
        second.append(
            (hi, sender.start(v, v, dev(p, step(q, 1))), sender.start(v, v, dev(p, step(q, 3))))
        )
        st.append((r0, r1))
    yield
    for (p, q, dev, blk, own), st in zip(flows, state):
        second, (r0, r1) = st[2], st[3]
        r0.wait_recv()
        r1.wait_recv()
        fa = step(p, 2)
        v = blk(fa, q, 0, half)
        second.append(
            (fa, sender.start(v, v, dev(p, step(q, 1))), sender.start(v, v, dev(p, step(q, 3))))
        )
    yield
    last = []
    for i in range(4):
        for (p, q, dev, blk, own), st in zip(flows, state):
            pa, c, d = st[2][i]
            c.wait_recv()
            v = blk(pa, step(q, 3), 0, quarter)
            last.append(sender.start(v, v, dev(p, step(q, 1))))
            d.wait_recv()
            v = blk(pa, step(q, 1), quarter, quarter)
            last.append(sender.start(v, v, dev(p, step(q, 3))))
    yield
    for copy in last:
        copy.wait_recv()


def entry_kernel(
    tok_ref,
    qkv_ref,
    meta_ref,
    tok_out,
    qkv_out,
    meta_out,
    tok_send,
    tok_recv,
    qkv_send,
    qkv_recv,
    meta_send,
    meta_recv,
    own_sem,
):
    row = lax.axis_index("row")
    col = lax.axis_index("col")
    x, y = col // 4, col % 4
    peers = [(row, (col + i) % 16) for i in range(1, 16)]
    own = [
        pltpu.make_async_copy(tok_ref, tok_out.at[col], own_sem.at[0]),
        pltpu.make_async_copy(qkv_ref, qkv_out.at[col], own_sem.at[1]),
        pltpu.make_async_copy(meta_ref, meta_out.at[col], own_sem.at[2]),
    ]
    for copy in own:
        copy.start()
    greet(peers)
    tok_sender = Sender(tok_send, tok_recv)
    qkv_sender = Sender(qkv_send, qkv_recv)
    meta_sender = Sender(meta_send, meta_recv)
    runs = [
        torus_gather(tok_ref, tok_out, row, x, y, tok_sender),
        torus_gather(qkv_ref, qkv_out, row, x, y, qkv_sender),
    ]
    for run in runs:
        next(run)
    for peer in peers:
        meta_sender.start(meta_ref, meta_out.at[col], peer)
    for _ in range(3):
        for run in runs:
            next(run)
    for run in runs:
        next(run, None)
    for copy in meta_sender.copies:
        copy.wait_recv()
    for sender in (tok_sender, qkv_sender, meta_sender):
        for copy in sender.copies:
            copy.wait_send()
    for copy in own:
        copy.wait()


def entry_gather(tok, qkv, meta):
    arrays = (tok, qkv, meta)
    return pl.pallas_call(
        entry_kernel,
        out_shape=[jax.ShapeDtypeStruct((16,) + a.shape, a.dtype) for a in arrays],
        in_specs=[HBM] * 3,
        out_specs=[HBM] * 3,
        scratch_shapes=[pltpu.SemaphoreType.DMA((40,))] * 4
        + [pltpu.SemaphoreType.DMA((15,))] * 2
        + [pltpu.SemaphoreType.DMA((3,))],
        compiler_params=pltpu.CompilerParams(collective_id=0, has_side_effects=True),
        name="entry_gather",
    )(tok, qkv, meta)


def home_kernel(in_ref, out_ref, send_sem, recv_sem, own_sem):
    row = lax.axis_index("row")
    col = lax.axis_index("col")
    peers = [(col + i) % 16 for i in range(1, 16)]
    own = pltpu.make_async_copy(in_ref.at[col], out_ref.at[col], own_sem)
    own.start()
    greet([(row, c) for c in peers])
    sender = Sender(send_sem, recv_sem)
    for c in peers:
        sender.start(in_ref.at[c], out_ref.at[col], (row, c))
    own.wait()
    for copy in sender.copies:
        copy.wait()


def send_home(packed):
    return pl.pallas_call(
        home_kernel,
        out_shape=jax.ShapeDtypeStruct(packed.shape, packed.dtype),
        in_specs=[HBM],
        out_specs=HBM,
        scratch_shapes=[
            pltpu.SemaphoreType.DMA((15,)),
            pltpu.SemaphoreType.DMA((15,)),
            pltpu.SemaphoreType.DMA,
        ],
        compiler_params=pltpu.CompilerParams(collective_id=1, has_side_effects=True),
        name="send_home",
    )(packed)


def scatter_kernel(
    part_ref, u_in, out_ref, u_ref, send_sem, recv_sem, u_send, u_recv, own_sem, mine, theirs
):
    row, col, z, core = row_place()
    tokens = mine.shape[1]
    half = tokens // 2
    loads = [
        pltpu.make_async_copy(part_ref.at[zz, core], mine.at[zz], own_sem.at[zz])
        for zz in range(4)
    ]
    for copy in loads:
        copy.start()
    greet(row_neighbours(col, z, core))
    sender = Sender(send_sem, recv_sem)
    partner = (z * 2 + 1 - core, col)
    order = [(z + 2) % 4, (z + 1) % 4, (z + 3) % 4, z]
    swaps = [
        sender.start(part_ref.at[zz, 1 - core], theirs.at[i], partner)
        for i, zz in enumerate(order)
    ]
    for copy in loads:
        copy.wait()
    up, down = ((z + 1) % 4) * 2 + core, ((z + 3) % 4) * 2 + core
    sent = []
    relayed = []
    for i, zz in enumerate(order):
        swaps[i].wait_recv()
        theirs[i] = (theirs[i].astype(f32) + mine[zz].astype(f32)).astype(bf16)
        if i == 0:
            top, bottom = pl.ds(0, half), pl.ds(half, half)
            relayed.append(sender.start(theirs.at[0, top], out_ref.at[4, top], (up, col)))
            relayed.append(sender.start(theirs.at[0, bottom], out_ref.at[4, bottom], (down, col)))
        elif i == 1:
            sent.append(sender.start(theirs.at[1], out_ref.at[1], (up, col)))
        elif i == 2:
            sent.append(sender.start(theirs.at[2], out_ref.at[2], (down, col)))
    u_sender = Sender(u_send, u_recv)
    keep = pltpu.make_async_copy(theirs.at[3], out_ref.at[3], own_sem.at[4])
    keep.start()
    relayed[0].wait_recv()
    sent.append(sender.start(out_ref.at[4, top], out_ref.at[0, top], (up, col)))
    relayed[1].wait_recv()
    sent.append(sender.start(out_ref.at[4, bottom], out_ref.at[0, bottom], (down, col)))
    ring_gather(u_ref, row, col, z, core, u_sender)
    for copy in sent:
        copy.wait_recv()
    for copy in sender.copies + u_sender.copies:
        copy.wait_send()
    keep.wait()


def row_scatter(part, u, cid):
    tokens = part.shape[2]
    out, u = pl.pallas_call(
        scatter_kernel,
        out_shape=[
            jax.ShapeDtypeStruct((5, tokens, 256), bf16),
            jax.ShapeDtypeStruct(u.shape, u.dtype),
        ],
        in_specs=[HBM] * 2,
        out_specs=[HBM] * 2,
        scratch_shapes=[
            pltpu.SemaphoreType.DMA((10,)),
            pltpu.SemaphoreType.DMA((10,)),
            pltpu.SemaphoreType.DMA((13,)),
            pltpu.SemaphoreType.DMA((13,)),
            pltpu.SemaphoreType.DMA((5,)),
            pltpu.VMEM((4, tokens, 256), bf16),
            pltpu.VMEM((4, tokens, 256), bf16),
        ],
        input_output_aliases={1: 1},
        compiler_params=pltpu.CompilerParams(collective_id=cid, has_side_effects=True),
        name="row_scatter",
    )(part, u)
    return out, u


def pieces(block, specs_of):
    return [pl.BlockSpec(block, functools.partial(specs_of, i)) for i in range(GRP)]


def by_slot(shape):
    rank = len(shape)

    def index(i, g, req, loc, length, row):
        return (loc[g * GRP + i],) + (0,) * rank

    return pieces((1,) + shape, index)


def by_group(shape):
    rank = len(shape)
    return pl.BlockSpec(shape, lambda g, req, loc, length, row: (0, g) + (0,) * (rank - 2))


def own_group(shape):
    return pl.BlockSpec(shape, lambda g, req, loc, length, row: (row[0], g, 0))


def rows_group(rows, width):
    return pl.BlockSpec((rows, width), lambda g, req, loc, length, row: (g, 0))


def whole(shape):
    rank = len(shape)
    return pl.BlockSpec(
        shape, lambda g, req, loc, length, row: (0,) * rank, pipeline_mode=pl.Buffered(1)
    )


def staged(kernel, name, table, in_specs, out_specs, out_shape, args):
    return pl.pallas_call(
        kernel,
        out_shape=out_shape,
        grid_spec=pltpu.PrefetchScalarGridSpec(
            num_scalar_prefetch=4,
            grid=(K // GRP,),
            in_specs=in_specs,
            out_specs=out_specs,
        ),
        compiler_params=pltpu.CompilerParams(vmem_limit_bytes=60 << 20),
        name=name,
    )(*table, *args)


def slot_rows(i):
    return slice(i * SLOT, (i + 1) * SLOT)


def rank_sum(buf, first):
    total = buf[0, first : first + RANK, :].astype(f32)
    for r in range(1, 8):
        total = total + buf[r, first : first + RANK, :].astype(f32)
    return total.astype(bf16)


def pack_kernel(req, loc, length, row, *refs):
    toks, shrinks, out = refs[:GRP], refs[GRP : 2 * GRP], refs[2 * GRP]
    for i in range(GRP):
        x = toks[i][0]
        out[0, slot_rows(i), :] = x
        u = dot_nt(x, shrinks[i][0]).astype(bf16)
        for j in range(3):
            out[0, TOK + j * RANK : TOK + (j + 1) * RANK, slot_rows(i)] = u[
                :, j * RANK : (j + 1) * RANK
            ]


def attend_kernel(req, loc, length, row, *refs):
    buf, weight = refs[0], refs[1]
    expands, shrinks, out = refs[2 : 2 + GRP], refs[2 + GRP : 2 + 2 * GRP], refs[-1]
    base = dot(buf[0, :TOK, :], weight[0:256, :])
    for r in range(1, 8):
        base = base + dot(buf[r, :TOK, :], weight[r * 256 : (r + 1) * 256, :])
    reduced = [rank_sum(buf, TOK + j * RANK) for j in range(3)]
    g = pl.program_id(0)
    lane = lax.broadcasted_iota(jnp.int32, (SLOT, SLOT), 1)
    for i in range(GRP):
        deltas = [
            dot(reduced[j][:, slot_rows(i)], expands[i][0, j]).astype(bf16).astype(f32)
            for j in range(3)
        ]
        valid = lane < length[g * GRP + i]
        contexts = []
        for h in range(2):
            q, k, v = [
                (
                    base[slot_rows(i), h * 384 + j * HD : h * 384 + (j + 1) * HD]
                    + lowrank_scale * deltas[j][:, h * HD : (h + 1) * HD]
                ).astype(bf16)
                for j in range(3)
            ]
            scores = dot_nt(q, k) / math.sqrt(HD)
            weights = jnp.where(valid, jnp.exp(scores), 0.0)
            probs = (weights / jnp.sum(weights, axis=1, keepdims=True)).astype(bf16)
            contexts.append(dot(probs, v).astype(bf16))
        context = jnp.concatenate(contexts, axis=1)
        out[0, slot_rows(i), :] = context
        out[0, TOK:, slot_rows(i)] = dot_nt(context, shrinks[i][0]).astype(bf16)


def stats_of(values):
    lane = lax.broadcasted_iota(jnp.int32, (TOK, 128), 1)
    one = jnp.sum(values, axis=1, keepdims=True)
    two = jnp.sum(values * values, axis=1, keepdims=True)
    flipped = jnp.where(lane < 64, one, two).T
    return jnp.concatenate([flipped[0:8], flipped[64:72]], axis=0)


def norm_of(values, stats, gain, shift):
    total = stats[0]
    for r in range(1, 8):
        total = total + stats[r]
    total = total * (1.0 / D)
    mean = total[0:1, :]
    square = total[8:9, :]
    factor = lax.rsqrt(square - mean * mean + eps)
    both = jnp.concatenate(
        [jnp.broadcast_to(mean, (8, TOK)), jnp.broadcast_to(factor, (8, TOK))] + [jnp.zeros((112, TOK), f32)],
        axis=0,
    ).T
    return (values - both[:, 0:1]) * both[:, 8:9] * gain + shift


def mix_kernel(req, loc, length, row, *refs):
    buf, tok, weight = refs[:3]
    expands, out, stats = refs[3 : 3 + GRP], refs[-2], refs[-1]
    base = dot(buf[0, :TOK, :], weight[0:256, :])
    for r in range(1, 8):
        base = base + dot(buf[r, :TOK, :], weight[r * 256 : (r + 1) * 256, :])
    reduced = rank_sum(buf, TOK)
    for i in range(GRP):
        delta = dot(reduced[:, slot_rows(i)], expands[i][0]).astype(bf16).astype(f32)
        out[slot_rows(i), :] = (
            tok[0, slot_rows(i), :].astype(f32) + base[slot_rows(i), :] + lowrank_scale * delta
        )
    stats[...] = stats_of(out[...])


def first_kernel(req, loc, length, row, *refs):
    pre, stats, gain, shift = refs[:4]
    shrinks, out = refs[4 : 4 + GRP], refs[-1]
    first = norm_of(pre[...], stats, gain[...], shift[...]).astype(bf16)
    out[0, :TOK, :] = first
    for i in range(GRP):
        out[0, TOK:, slot_rows(i)] = dot_nt(first[slot_rows(i), :], shrinks[i][0]).astype(bf16)


def gelu(v):
    return 0.5 * v * (1.0 + jnp.tanh(math.sqrt(2.0 / math.pi) * (v + 0.044715 * (v * v * v))))


def hidden_kernel(req, loc, length, row, *refs):
    buf, widen, contract = refs[:3]
    expands, shrinks = refs[3 : 3 + GRP], refs[3 + GRP : 3 + 2 * GRP]
    part, ud = refs[-2], refs[-1]
    base = dot(buf[0, :TOK, :], widen[0:256, :])
    for r in range(1, 8):
        base = base + dot(buf[r, :TOK, :], widen[r * 256 : (r + 1) * 256, :])
    reduced = rank_sum(buf, TOK)
    rows = []
    for i in range(GRP):
        delta = dot(reduced[:, slot_rows(i)], expands[i][0]).astype(bf16).astype(f32)
        hidden = gelu(base[slot_rows(i), :] + lowrank_scale * delta).astype(bf16)
        rows.append(hidden)
        ud[0, :, slot_rows(i)] = dot_nt(hidden, shrinks[i][0]).astype(bf16)
    hidden = jnp.concatenate(rows, axis=0)
    for r in range(8):
        part[r // 2, r % 2] = dot_nt(hidden, contract[r * 256 : (r + 1) * 256, :]).astype(bf16)


def second_kernel(req, loc, length, row, *refs):
    summed, ud, first = refs[:3]
    expands, out, stats = refs[3 : 3 + GRP], refs[-2], refs[-1]
    reduced = rank_sum(ud, 0)
    base = summed[0].astype(f32)
    for r in range(1, 4):
        base = base + summed[r].astype(f32)
    for i in range(GRP):
        delta = dot(reduced[:, slot_rows(i)], expands[i][0]).astype(bf16).astype(f32)
        out[slot_rows(i), :] = (
            first[0, slot_rows(i), :].astype(f32) + base[slot_rows(i), :] + lowrank_scale * delta
        )
    stats[...] = stats_of(out[...])


def last_kernel(req, loc, length, row, pre, stats, gain, shift, out):
    out[...] = norm_of(pre[...], stats, gain[...], shift[...]).astype(bf16)


def shards(
    tokens,
    lengths,
    adapter_ids,
    adapter_place,
    attention_qkv_weight,
    attention_out_weight,
    widen_weight,
    contract_weight,
    first_gain,
    first_shift,
    second_gain,
    second_shift,
    attend_shrink,
    attend_expand,
    output_shrink,
    output_expand,
    upward_shrink,
    upward_expand,
    downward_shrink,
    downward_expand,
):
    i32 = jnp.int32
    col = lax.axis_index("col")
    row = lax.axis_index("row")
    stored = attend_shrink.shape[0]
    match = adapter_ids[:, None] == jnp.arange(adapter_place.shape[0], dtype=i32)[None, :]
    position = jnp.sum(jnp.where(match, adapter_place[None, :], 0), axis=1)
    meta = jnp.zeros((8, 128), i32)
    meta = meta.at[0, :REQ_COL].set(position).at[1, :REQ_COL].set(lengths)
    tok_all, qkv_all, meta_all = entry_gather(tokens.T, attention_qkv_weight, meta)
    out_all = lax.all_gather(attention_out_weight, "col", axis=0, tiled=True)
    widen_all = lax.all_gather(widen_weight, "col", axis=0, tiled=True)
    contract_all = lax.all_gather(contract_weight, "col", axis=0, tiled=True)
    qkv_all = qkv_all.reshape(D, -1)
    tok_all = tok_all.reshape(64, SLOT, 256)

    requests = 64
    position = meta_all[:, 0, :REQ_COL].reshape(requests)
    length = meta_all[:, 1, :REQ_COL].reshape(requests)
    owner, local = position // stored, position % stored
    n = jnp.arange(requests, dtype=i32)
    same = (owner[None, :] == owner[:, None]) & (n[None, :] < n[:, None])
    rank = jnp.sum(same.astype(i32), axis=1)
    near = jnp.sum((same & (n[None, :] // REQ_COL == n[:, None] // REQ_COL)).astype(i32), axis=1)
    waves = (jnp.max(rank) + K) // K
    most = -(-32 // K)
    slots = jnp.arange(most * K, dtype=i32)
    mine = owner == col
    hit = mine[None, :] & (rank[None, :] == slots[:, None])
    req = jnp.sum(jnp.where(hit, n[None, :], 0), axis=1)
    loc = jnp.sum(jnp.where(hit, local[None, :], 0), axis=1)
    lens = jnp.maximum(jnp.sum(jnp.where(hit, length[None, :], 0), axis=1), 1)
    pair = jnp.arange(32, dtype=i32)
    out_hit = mine[None, :] & ((n // REQ_COL * 2 + near)[None, :] == pair[:, None])
    out_slot = jnp.sum(jnp.where(out_hit, rank[None, :], 0), axis=1)
    home_n = col * REQ_COL + jnp.arange(REQ_COL, dtype=i32)
    home_hit = home_n[:, None] == n[None, :]
    home_from = jnp.sum(jnp.where(home_hit, (owner * 2 + near)[None, :], 0), axis=1)
    row_id = row.astype(i32)[None]
    groups = K // GRP
    tall = K * SLOT
    gain1 = first_gain[None, :]
    shift1 = lax.dynamic_slice_in_dim(first_shift, row * 256, 256, 0)[None, :]
    gain2 = lax.dynamic_slice_in_dim(second_gain, row * 256, 256, 0)[None, :]
    shift2 = lax.dynamic_slice_in_dim(second_shift, row * 256, 256, 0)[None, :]

    def wave(w):
        table = tuple(
            lax.dynamic_slice_in_dim(t, w * K, K, 0) for t in (req, loc, lens)
        ) + (row_id,)

        def shape(*dims, dtype=bf16):
            return jax.ShapeDtypeStruct(dims, dtype)

        def token_slot(i, g, req, loc, length, row):
            return (req[g * GRP + i], 0, 0)

        high = TOK + 3 * RANK
        low = TOK + RANK
        buf1 = staged(
            pack_kernel,
            "pack",
            table,
            pieces((1, SLOT, 256), token_slot) + by_slot((3 * RANK, 256)),
            own_group((1, high, 256)),
            shape(8, groups * high, 256),
            [tok_all] * GRP + [attend_shrink] * GRP,
        )
        buf1 = row_gather(buf1, 2)
        buf2 = staged(
            attend_kernel,
            "attend",
            table,
            [by_group((8, high, 256)), whole((D, 768))]
            + by_slot((3, RANK, 256))
            + by_slot((RANK, 256)),
            own_group((1, low, 256)),
            shape(8, groups * low, 256),
            [buf1, qkv_all] + [attend_expand] * GRP + [output_shrink] * GRP,
        )
        buf2 = row_gather(buf2, 3)
        pre, stats = staged(
            mix_kernel,
            "mix",
            table,
            [by_group((8, low, 256)), own_group((1, high, 256)), whole((D, 256))]
            + by_slot((RANK, 256)),
            [rows_group(TOK, 256), rows_group(16, 256)],
            [shape(tall, 256, dtype=f32), shape(groups * 16, 256, dtype=f32)],
            [buf2, buf1, out_all] + [output_expand] * GRP,
        )
        stats = stat_gather(stats, 4)
        buf3 = staged(
            first_kernel,
            "first",
            table,
            [rows_group(TOK, 256), by_group((8, 16, 256)), whole((1, 256)), whole((1, 256))]
            + by_slot((RANK, 256)),
            own_group((1, low, 256)),
            shape(8, groups * low, 256),
            [pre, stats, gain1, shift1] + [upward_shrink] * GRP,
        )
        buf3 = row_gather(buf3, 3)
        part, ud = staged(
            hidden_kernel,
            "hidden",
            table,
            [by_group((8, low, 256)), whole((D, 1024)), whole((D, 1024))]
            + by_slot((RANK, 1024))
            + by_slot((RANK, 1024)),
            [
                pl.BlockSpec((4, 2, TOK, 256), lambda g, req, loc, length, row: (0, 0, g, 0)),
                own_group((1, RANK, 256)),
            ],
            [shape(4, 2, tall, 256), shape(8, groups * RANK, 256)],
            [buf3, widen_all, contract_all]
            + [upward_expand] * GRP
            + [downward_shrink] * GRP,
        )
        summed, ud = row_scatter(part, ud, 5)
        pre, stats = staged(
            second_kernel,
            "second",
            table,
            [by_group((4, TOK, 256)), by_group((8, RANK, 256)), own_group((1, low, 256))]
            + by_slot((RANK, 256)),
            [rows_group(TOK, 256), rows_group(16, 256)],
            [shape(tall, 256, dtype=f32), shape(groups * 16, 256, dtype=f32)],
            [summed, ud, buf3] + [downward_expand] * GRP,
        )
        stats = stat_gather(stats, 4)
        return staged(
            last_kernel,
            "last",
            table,
            [rows_group(TOK, 256), by_group((8, 16, 256)), whole((1, 256)), whole((1, 256))],
            rows_group(TOK, 256),
            shape(tall, 256),
            [pre, stats, gain2, shift2],
        )

    result = wave(0)

    def quick(result):
        return jnp.take(result.reshape(K, SLOT, 256), jnp.minimum(out_slot, K - 1), axis=0)

    def longer(result):
        held = jnp.zeros((most, tall, 256), bf16)
        held = lax.dynamic_update_index_in_dim(held, result, 0, 0)
        held = lax.fori_loop(
            1, waves, lambda w, h: lax.dynamic_update_index_in_dim(h, wave(w), w, 0), held
        )
        return jnp.take(held.reshape(most * K, SLOT, 256), out_slot, axis=0)

    packed = lax.cond(waves > 1, longer, quick, result)
    arrived = send_home(packed.reshape(16, 2 * SLOT, 256))
    own = jnp.take(arrived.reshape(32, SLOT, 256), home_from, axis=0).reshape(TOK, 256)
    wide = lax.all_gather(own.T, "row", axis=0, tiled=True)
    return wide


def solution(mesh):
    return jax.shard_map(
        shards,
        mesh=mesh,
        in_specs=(
            P("row", "col"),
            P("col"),
            P("col"),
            P(),
            P("col", "row"),
            P("col", "row"),
            P("col", "row"),
            P("col", "row"),
            P("row"),
            P(),
            P(),
            P(),
            P("col", None, "row"),
            P("col", None, None, "row"),
            P("col", None, "row"),
            P("col", None, "row"),
            P("col", None, "row"),
            P("col", None, "row"),
            P("col", None, "row"),
            P("col", None, "row"),
        ),
        out_specs=P(None, "col"),
        check_vma=False,
    )
```

```python
import functools
import math

import jax
import jax.numpy as jnp
from jax import lax
from jax.experimental import pallas as pl
from jax.experimental.pallas import tpu as pltpu
from jax.sharding import PartitionSpec as P

D = 2048
HD = 128
SLOT = 64
RANK = 64
GRP = 4
TOK = GRP * SLOT
K = 12
REQ_COL = 4

eps = 1e-12
lowrank_scale = 0.5

MESH = pl.DeviceIdType.MESH
HBM = pl.BlockSpec(memory_space=pl.ANY)
NT = (((1,), (1,)), ((), ()))
f32 = jnp.float32
bf16 = jnp.bfloat16


def dot(a, b):
    return jnp.dot(a, b, preferred_element_type=f32)


def dot_nt(a, b):
    return lax.dot_general(a, b, NT, preferred_element_type=f32)


def greet(peers):
    barrier = pltpu.get_barrier_semaphore()
    for peer in peers:
        pl.semaphore_signal(barrier, inc=1, device_id=peer, device_id_type=MESH)
    pl.semaphore_wait(barrier, len(peers))


class Sender:
    def __init__(self, send_sem, recv_sem):
        self.send_sem, self.recv_sem = send_sem, recv_sem
        self.copies = []

    def start(self, src, dst, peer):
        i = len(self.copies)
        copy = pltpu.make_async_remote_copy(
            src_ref=src,
            dst_ref=dst,
            send_sem=self.send_sem.at[i],
            recv_sem=self.recv_sem.at[i],
            device_id=peer,
            device_id_type=MESH,
        )
        copy.start()
        self.copies.append(copy)
        return copy


def row_place():
    row = lax.axis_index("row")
    col = lax.axis_index("col")
    z, core = row // 2, row % 2
    return row, col, z, core


def ring_gather(buf, row, col, z, core, sender):
    half = buf.shape[1] // 2
    up, down = (z + 1) % 4, (z + 3) % 4
    far = (z + 2) % 4

    def part(zz, h):
        return buf.at[zz * 2 + core, pl.ds(h * half, half)]

    def dev(zz):
        return (zz * 2 + core, col)

    partner = (z * 2 + 1 - core, col)
    a0 = sender.start(part(z, 0), part(z, 0), dev(up))
    b1 = sender.start(part(z, 1), part(z, 1), dev(down))
    a1 = sender.start(part(z, 1), part(z, 1), dev(up))
    b0 = sender.start(part(z, 0), part(z, 0), dev(down))
    own = sender.start(buf.at[row], buf.at[row], partner)
    rest = [own]

    def across(zz, h):
        rest.append(sender.start(part(zz, h), part(zz, h), partner))

    yield
    a0.wait_recv()
    r0 = sender.start(part(down, 0), part(down, 0), dev(up))
    across(down, 0)
    b1.wait_recv()
    r1 = sender.start(part(up, 1), part(up, 1), dev(down))
    across(up, 1)
    yield
    a1.wait_recv()
    across(down, 1)
    b0.wait_recv()
    across(up, 0)
    yield
    r0.wait_recv()
    across(far, 0)
    r1.wait_recv()
    across(far, 1)
    yield
    for copy in rest:
        copy.wait_recv()


def finish(run):
    for _ in run:
        pass


def row_neighbours(col, z, core):
    return [
        (((z + 1) % 4) * 2 + core, col),
        (((z + 3) % 4) * 2 + core, col),
        (z * 2 + 1 - core, col),
    ]


def row_gather_kernel(in_ref, out_ref, send_sem, recv_sem):
    row, col, z, core = row_place()
    greet(row_neighbours(col, z, core))
    sender = Sender(send_sem, recv_sem)
    finish(ring_gather(out_ref, row, col, z, core, sender))
    for copy in sender.copies:
        copy.wait_send()


def row_gather(buf, cid):
    return pl.pallas_call(
        row_gather_kernel,
        out_shape=jax.ShapeDtypeStruct(buf.shape, buf.dtype),
        in_specs=[HBM],
        out_specs=HBM,
        scratch_shapes=[pltpu.SemaphoreType.DMA((13,)), pltpu.SemaphoreType.DMA((13,))],
        input_output_aliases={0: 0},
        compiler_params=pltpu.CompilerParams(collective_id=cid, has_side_effects=True),
        name="row_gather",
    )(buf)


def stat_gather_kernel(in_ref, out_ref, send_sem, recv_sem, own_sem):
    row = lax.axis_index("row")
    col = lax.axis_index("col")
    peers = [((row + i) % 8, col) for i in range(1, 8)]
    own = pltpu.make_async_copy(in_ref, out_ref.at[row], own_sem)
    own.start()
    greet(peers)
    sender = Sender(send_sem, recv_sem)
    for peer in peers:
        sender.start(in_ref, out_ref.at[row], peer)
    own.wait()
    for copy in sender.copies:
        copy.wait()


def stat_gather(part, cid):
    return pl.pallas_call(
        stat_gather_kernel,
        out_shape=jax.ShapeDtypeStruct((8,) + part.shape, part.dtype),
        in_specs=[pl.BlockSpec(memory_space=pltpu.VMEM)],
        out_specs=pl.BlockSpec(memory_space=pltpu.VMEM),
        scratch_shapes=[
            pltpu.SemaphoreType.DMA((7,)),
            pltpu.SemaphoreType.DMA((7,)),
            pltpu.SemaphoreType.DMA,
        ],
        compiler_params=pltpu.CompilerParams(collective_id=cid, has_side_effects=True),
        name="stat_gather",
    )(part)


def torus_gather(src, dst, row, x, y, sender):
    rows = src.shape[0]
    half, quarter = rows // 2, rows // 4

    def step(p, d):
        return (p + d) % 4

    flows = []
    for first in (0, 1):
        base = first * half

        def at(a, b, first=first):
            return (a * 4 + b) if first == 0 else (b * 4 + a)

        p, q = (x, y) if first == 0 else (y, x)

        def dev(a, b, at=at):
            return (row, at(a, b))

        def blk(a, b, lo, n, at=at, base=base):
            return dst.at[at(a, b), pl.ds(base + lo, n)]

        own = src.at[pl.ds(base, half)]
        flows.append((p, q, dev, blk, own))

    state = []
    for p, q, dev, blk, own in flows:
        here = blk(p, q, 0, half)
        a = sender.start(own, here, dev(step(p, 1), q))
        b = sender.start(own, here, dev(step(p, 3), q))
        c = sender.start(own, here, dev(p, step(q, 1)))
        d = sender.start(own, here, dev(p, step(q, 3)))
        state.append([a, b, [(p, c, d)]])
    yield
    relays = []
    for (p, q, dev, blk, own), st in zip(flows, state):
        a, b, second = st
        lo, hi = step(p, 3), step(p, 1)
        a.wait_recv()
        v = blk(lo, q, 0, quarter)
        r0 = sender.start(v, v, dev(step(p, 1), q))
        v = blk(lo, q, 0, half)
        second.append(
            (lo, sender.start(v, v, dev(p, step(q, 1))), sender.start(v, v, dev(p, step(q, 3))))
        )
        b.wait_recv()
        v = blk(hi, q, quarter, quarter)
        r1 = sender.start(v, v, dev(step(p, 3), q))
        v = blk(hi, q, 0, half)
        second.append(
            (hi, sender.start(v, v, dev(p, step(q, 1))), sender.start(v, v, dev(p, step(q, 3))))
        )
        st.append((r0, r1))
    yield
    for (p, q, dev, blk, own), st in zip(flows, state):
        second, (r0, r1) = st[2], st[3]
        r0.wait_recv()
        r1.wait_recv()
        fa = step(p, 2)
        v = blk(fa, q, 0, half)
        second.append(
            (fa, sender.start(v, v, dev(p, step(q, 1))), sender.start(v, v, dev(p, step(q, 3))))
        )
    yield
    last = []
    for i in range(4):
        for (p, q, dev, blk, own), st in zip(flows, state):
            pa, c, d = st[2][i]
            c.wait_recv()
            v = blk(pa, step(q, 3), 0, quarter)
            last.append(sender.start(v, v, dev(p, step(q, 1))))
            d.wait_recv()
            v = blk(pa, step(q, 1), quarter, quarter)
            last.append(sender.start(v, v, dev(p, step(q, 3))))
    yield
    for copy in last:
        copy.wait_recv()


def torus_neighbours(row, x, y):
    return [
        (row, (x + 1) % 4 * 4 + y),
        (row, (x + 3) % 4 * 4 + y),
        (row, x * 4 + (y + 1) % 4),
        (row, x * 4 + (y + 3) % 4),
    ]


def entry_kernel(
    tok_ref, meta_ref, tok_out, meta_out, tok_send, tok_recv, meta_send, meta_recv, own_sem
):
    row = lax.axis_index("row")
    col = lax.axis_index("col")
    x, y = col // 4, col % 4
    peers = [(row, (col + i) % 16) for i in range(1, 16)]
    own = [
        pltpu.make_async_copy(tok_ref, tok_out.at[col], own_sem.at[0]),
        pltpu.make_async_copy(meta_ref, meta_out.at[col], own_sem.at[1]),
    ]
    for copy in own:
        copy.start()
    greet(peers)
    tok_sender = Sender(tok_send, tok_recv)
    meta_sender = Sender(meta_send, meta_recv)
    run = torus_gather(tok_ref, tok_out, row, x, y, tok_sender)
    next(run)
    for peer in peers:
        meta_sender.start(meta_ref, meta_out.at[col], peer)
    finish(run)
    for copy in meta_sender.copies:
        copy.wait_recv()
    for sender in (tok_sender, meta_sender):
        for copy in sender.copies:
            copy.wait_send()
    for copy in own:
        copy.wait()


def entry_gather(tok, meta):
    arrays = (tok, meta)
    return pl.pallas_call(
        entry_kernel,
        out_shape=[jax.ShapeDtypeStruct((16,) + a.shape, a.dtype) for a in arrays],
        in_specs=[HBM] * 2,
        out_specs=[HBM] * 2,
        scratch_shapes=[pltpu.SemaphoreType.DMA((40,))] * 2
        + [pltpu.SemaphoreType.DMA((15,))] * 2
        + [pltpu.SemaphoreType.DMA((2,))],
        compiler_params=pltpu.CompilerParams(collective_id=0, has_side_effects=True),
        name="entry_gather",
    )(tok, meta)


def wide_gather_kernel(
    buf_in, qkv_ref, out_ref, buf, qkv_all, out_all,
    send_sem, recv_sem, q_send, q_recv, o_send, o_recv, own_sem
):
    row, col, z, core = row_place()
    x, y = col // 4, col % 4
    own = [
        pltpu.make_async_copy(qkv_ref, qkv_all.at[col], own_sem.at[0]),
        pltpu.make_async_copy(out_ref, out_all.at[col], own_sem.at[1]),
    ]
    for copy in own:
        copy.start()
    greet(row_neighbours(col, z, core) + torus_neighbours(row, x, y))
    senders = [Sender(send_sem, recv_sem), Sender(q_send, q_recv), Sender(o_send, o_recv)]
    ring = ring_gather(buf, row, col, z, core, senders[0])
    qkv = torus_gather(qkv_ref, qkv_all, row, x, y, senders[1])
    out = torus_gather(out_ref, out_all, row, x, y, senders[2])
    for run in (ring, qkv, qkv, qkv, ring, qkv, out, out, out, out, ring):
        next(run)
    for run in (ring, qkv, out):
        finish(run)
    for sender in senders:
        for copy in sender.copies:
            copy.wait_send()
    for copy in own:
        copy.wait()


def wide_gather(buf, qkv, out, cid):
    return pl.pallas_call(
        wide_gather_kernel,
        out_shape=[
            jax.ShapeDtypeStruct(buf.shape, buf.dtype),
            jax.ShapeDtypeStruct((16,) + qkv.shape, qkv.dtype),
            jax.ShapeDtypeStruct((16,) + out.shape, out.dtype),
        ],
        in_specs=[HBM] * 3,
        out_specs=[HBM] * 3,
        scratch_shapes=[pltpu.SemaphoreType.DMA((13,))] * 2
        + [pltpu.SemaphoreType.DMA((40,))] * 4
        + [pltpu.SemaphoreType.DMA((2,))],
        input_output_aliases={0: 0},
        compiler_params=pltpu.CompilerParams(collective_id=cid, has_side_effects=True),
        name="wide_gather",
    )(buf, qkv, out)


def exit_kernel(pick, in_ref, out_ref, send_sem, recv_sem, r_send, r_recv, own_sem, arrived):
    row, col, z, core = row_place()
    peers = [(col + i) % 16 for i in range(1, 16)]
    here = arrived.at[pl.ds(col * 2, 2)]
    own = pltpu.make_async_copy(in_ref.at[col], here, own_sem)
    own.start()
    greet([(row, c) for c in peers] + row_neighbours(col, z, core))
    sender = Sender(send_sem, recv_sem)
    for c in peers:
        sender.start(in_ref.at[c], here, (row, c))
    own.wait()
    for copy in sender.copies:
        copy.wait_recv()
    mine = jnp.concatenate([arrived[pick[i]] for i in range(REQ_COL)], axis=0)
    out_ref[row] = mine.T
    r_sender = Sender(r_send, r_recv)
    finish(ring_gather(out_ref, row, col, z, core, r_sender))
    for copy in sender.copies + r_sender.copies:
        copy.wait_send()


def send_home(packed, pick):
    return pl.pallas_call(
        exit_kernel,
        out_shape=jax.ShapeDtypeStruct((8, 256, TOK), packed.dtype),
        in_specs=[pl.BlockSpec(memory_space=pltpu.SMEM), HBM],
        out_specs=pl.BlockSpec(memory_space=pltpu.VMEM),
        scratch_shapes=[
            pltpu.SemaphoreType.DMA((15,)),
            pltpu.SemaphoreType.DMA((15,)),
            pltpu.SemaphoreType.DMA((13,)),
            pltpu.SemaphoreType.DMA((13,)),
            pltpu.SemaphoreType.DMA,
            pltpu.VMEM((32, SLOT, 256), packed.dtype),
        ],
        compiler_params=pltpu.CompilerParams(collective_id=1, has_side_effects=True),
        name="send_home",
    )(pick, packed)


def scatter_kernel(
    part_ref, u_in, out_ref, u_ref, send_sem, recv_sem, u_send, u_recv, own_sem, mine, theirs
):
    row, col, z, core = row_place()
    tokens = mine.shape[1]
    half = tokens // 2
    loads = [
        pltpu.make_async_copy(part_ref.at[zz, core], mine.at[zz], own_sem.at[zz])
        for zz in range(4)
    ]
    for copy in loads:
        copy.start()
    greet(row_neighbours(col, z, core))
    sender = Sender(send_sem, recv_sem)
    partner = (z * 2 + 1 - core, col)
    order = [(z + 2) % 4, (z + 1) % 4, (z + 3) % 4, z]
    swaps = [
        sender.start(part_ref.at[zz, 1 - core], theirs.at[i], partner)
        for i, zz in enumerate(order)
    ]
    for copy in loads:
        copy.wait()
    up, down = ((z + 1) % 4) * 2 + core, ((z + 3) % 4) * 2 + core
    sent = []
    relayed = []
    for i, zz in enumerate(order):
        swaps[i].wait_recv()
        theirs[i] = (theirs[i].astype(f32) + mine[zz].astype(f32)).astype(bf16)
        if i == 0:
            top, bottom = pl.ds(0, half), pl.ds(half, half)
            relayed.append(sender.start(theirs.at[0, top], out_ref.at[4, top], (up, col)))
            relayed.append(sender.start(theirs.at[0, bottom], out_ref.at[4, bottom], (down, col)))
        elif i == 1:
            sent.append(sender.start(theirs.at[1], out_ref.at[1], (up, col)))
        elif i == 2:
            sent.append(sender.start(theirs.at[2], out_ref.at[2], (down, col)))
    u_sender = Sender(u_send, u_recv)
    keep = pltpu.make_async_copy(theirs.at[3], out_ref.at[3], own_sem.at[4])
    keep.start()
    relayed[0].wait_recv()
    sent.append(sender.start(out_ref.at[4, top], out_ref.at[0, top], (up, col)))
    relayed[1].wait_recv()
    sent.append(sender.start(out_ref.at[4, bottom], out_ref.at[0, bottom], (down, col)))
    finish(ring_gather(u_ref, row, col, z, core, u_sender))
    for copy in sent:
        copy.wait_recv()
    for copy in sender.copies + u_sender.copies:
        copy.wait_send()
    keep.wait()


def row_scatter(part, u, cid):
    tokens = part.shape[2]
    out, u = pl.pallas_call(
        scatter_kernel,
        out_shape=[
            jax.ShapeDtypeStruct((5, tokens, 256), bf16),
            jax.ShapeDtypeStruct(u.shape, u.dtype),
        ],
        in_specs=[HBM] * 2,
        out_specs=[HBM] * 2,
        scratch_shapes=[
            pltpu.SemaphoreType.DMA((10,)),
            pltpu.SemaphoreType.DMA((10,)),
            pltpu.SemaphoreType.DMA((13,)),
            pltpu.SemaphoreType.DMA((13,)),
            pltpu.SemaphoreType.DMA((5,)),
            pltpu.VMEM((4, tokens, 256), bf16),
            pltpu.VMEM((4, tokens, 256), bf16),
        ],
        input_output_aliases={1: 1},
        compiler_params=pltpu.CompilerParams(collective_id=cid, has_side_effects=True),
        name="row_scatter",
    )(part, u)
    return out, u


def pieces(block, specs_of):
    return [pl.BlockSpec(block, functools.partial(specs_of, i)) for i in range(GRP)]


def by_slot(shape):
    rank = len(shape)

    def index(i, g, req, loc, length, row):
        return (loc[g * GRP + i],) + (0,) * rank

    return pieces((1,) + shape, index)


def by_group(shape):
    rank = len(shape)
    return pl.BlockSpec(shape, lambda g, req, loc, length, row: (0, g) + (0,) * (rank - 2))


def own_group(shape):
    return pl.BlockSpec(shape, lambda g, req, loc, length, row: (row[0], g, 0))


def rows_group(rows, width):
    return pl.BlockSpec((rows, width), lambda g, req, loc, length, row: (g, 0))


def whole(shape):
    rank = len(shape)
    return pl.BlockSpec(
        shape, lambda g, req, loc, length, row: (0,) * rank, pipeline_mode=pl.Buffered(1)
    )


def staged(kernel, name, table, in_specs, out_specs, out_shape, args):
    return pl.pallas_call(
        kernel,
        out_shape=out_shape,
        grid_spec=pltpu.PrefetchScalarGridSpec(
            num_scalar_prefetch=4,
            grid=(K // GRP,),
            in_specs=in_specs,
            out_specs=out_specs,
        ),
        compiler_params=pltpu.CompilerParams(vmem_limit_bytes=60 << 20),
        name=name,
    )(*table, *args)


def slot_rows(i):
    return slice(i * SLOT, (i + 1) * SLOT)


def rank_sum(buf, first):
    total = buf[0, first : first + RANK, :].astype(f32)
    for r in range(1, 8):
        total = total + buf[r, first : first + RANK, :].astype(f32)
    return total.astype(bf16)


def pack_kernel(req, loc, length, row, *refs):
    toks, shrinks, out = refs[:GRP], refs[GRP : 2 * GRP], refs[2 * GRP]
    for i in range(GRP):
        x = toks[i][0]
        out[0, slot_rows(i), :] = x
        u = dot_nt(x, shrinks[i][0]).astype(bf16)
        for j in range(3):
            out[0, TOK + j * RANK : TOK + (j + 1) * RANK, slot_rows(i)] = u[
                :, j * RANK : (j + 1) * RANK
            ]


def attend_kernel(req, loc, length, row, *refs):
    buf, weight = refs[0], refs[1]
    expands, shrinks, out = refs[2 : 2 + GRP], refs[2 + GRP : 2 + 2 * GRP], refs[-1]
    base = dot(buf[0, :TOK, :], weight[0:256, :])
    for r in range(1, 8):
        base = base + dot(buf[r, :TOK, :], weight[r * 256 : (r + 1) * 256, :])
    reduced = [rank_sum(buf, TOK + j * RANK) for j in range(3)]
    g = pl.program_id(0)
    lane = lax.broadcasted_iota(jnp.int32, (SLOT, SLOT), 1)
    for i in range(GRP):
        deltas = [
            dot(reduced[j][:, slot_rows(i)], expands[i][0, j]).astype(bf16).astype(f32)
            for j in range(3)
        ]
        valid = lane < length[g * GRP + i]
        contexts = []
        for h in range(2):
            q, k, v = [
                (
                    base[slot_rows(i), h * 384 + j * HD : h * 384 + (j + 1) * HD]
                    + lowrank_scale * deltas[j][:, h * HD : (h + 1) * HD]
                ).astype(bf16)
                for j in range(3)
            ]
            scores = dot_nt(q, k) / math.sqrt(HD)
            weights = jnp.where(valid, jnp.exp(scores), 0.0)
            probs = (weights / jnp.sum(weights, axis=1, keepdims=True)).astype(bf16)
            contexts.append(dot(probs, v).astype(bf16))
        context = jnp.concatenate(contexts, axis=1)
        out[0, slot_rows(i), :] = context
        out[0, TOK:, slot_rows(i)] = dot_nt(context, shrinks[i][0]).astype(bf16)


def stats_of(values):
    lane = lax.broadcasted_iota(jnp.int32, (TOK, 128), 1)
    one = jnp.sum(values, axis=1, keepdims=True)
    two = jnp.sum(values * values, axis=1, keepdims=True)
    flipped = jnp.where(lane < 64, one, two).T
    return jnp.concatenate([flipped[0:8], flipped[64:72]], axis=0)


def norm_of(values, stats, gain, shift):
    total = stats[0]
    for r in range(1, 8):
        total = total + stats[r]
    total = total * (1.0 / D)
    mean = total[0:1, :]
    square = total[8:9, :]
    factor = lax.rsqrt(square - mean * mean + eps)
    both = jnp.concatenate(
        [jnp.broadcast_to(mean, (8, TOK)), jnp.broadcast_to(factor, (8, TOK))] + [jnp.zeros((112, TOK), f32)],
        axis=0,
    ).T
    return (values - both[:, 0:1]) * both[:, 8:9] * gain + shift


def mix_kernel(req, loc, length, row, *refs):
    buf, tok, weight = refs[:3]
    expands, out, stats = refs[3 : 3 + GRP], refs[-2], refs[-1]
    base = dot(buf[0, :TOK, :], weight[0:256, :])
    for r in range(1, 8):
        base = base + dot(buf[r, :TOK, :], weight[r * 256 : (r + 1) * 256, :])
    reduced = rank_sum(buf, TOK)
    for i in range(GRP):
        delta = dot(reduced[:, slot_rows(i)], expands[i][0]).astype(bf16).astype(f32)
        out[slot_rows(i), :] = (
            tok[0, slot_rows(i), :].astype(f32) + base[slot_rows(i), :] + lowrank_scale * delta
        )
    stats[...] = stats_of(out[...])


def first_kernel(req, loc, length, row, *refs):
    pre, stats, gain, shift = refs[:4]
    shrinks, out = refs[4 : 4 + GRP], refs[-1]
    first = norm_of(pre[...], stats, gain[...], shift[...]).astype(bf16)
    out[0, :TOK, :] = first
    for i in range(GRP):
        out[0, TOK:, slot_rows(i)] = dot_nt(first[slot_rows(i), :], shrinks[i][0]).astype(bf16)


def gelu(v):
    return 0.5 * v * (1.0 + jnp.tanh(math.sqrt(2.0 / math.pi) * (v + 0.044715 * (v * v * v))))


def hidden_kernel(req, loc, length, row, *refs):
    buf, widen, contract = refs[:3]
    expands, shrinks = refs[3 : 3 + GRP], refs[3 + GRP : 3 + 2 * GRP]
    part, ud = refs[-2], refs[-1]
    base = dot(buf[0, :TOK, :], widen[0:256, :])
    for r in range(1, 8):
        base = base + dot(buf[r, :TOK, :], widen[r * 256 : (r + 1) * 256, :])
    reduced = rank_sum(buf, TOK)
    rows = []
    for i in range(GRP):
        delta = dot(reduced[:, slot_rows(i)], expands[i][0]).astype(bf16).astype(f32)
        hidden = gelu(base[slot_rows(i), :] + lowrank_scale * delta).astype(bf16)
        rows.append(hidden)
        ud[0, :, slot_rows(i)] = dot_nt(hidden, shrinks[i][0]).astype(bf16)
    hidden = jnp.concatenate(rows, axis=0)
    for r in range(8):
        part[r // 2, r % 2] = dot_nt(hidden, contract[r * 256 : (r + 1) * 256, :]).astype(bf16)


def second_kernel(req, loc, length, row, *refs):
    summed, ud, first = refs[:3]
    expands, out, stats = refs[3 : 3 + GRP], refs[-2], refs[-1]
    reduced = rank_sum(ud, 0)
    base = summed[0].astype(f32)
    for r in range(1, 4):
        base = base + summed[r].astype(f32)
    for i in range(GRP):
        delta = dot(reduced[:, slot_rows(i)], expands[i][0]).astype(bf16).astype(f32)
        out[slot_rows(i), :] = (
            first[0, slot_rows(i), :].astype(f32) + base[slot_rows(i), :] + lowrank_scale * delta
        )
    stats[...] = stats_of(out[...])


def last_kernel(req, loc, length, row, pre, stats, gain, shift, out):
    out[...] = norm_of(pre[...], stats, gain[...], shift[...]).astype(bf16)


def shards(
    tokens,
    lengths,
    adapter_ids,
    adapter_place,
    attention_qkv_weight,
    attention_out_weight,
    widen_weight,
    contract_weight,
    first_gain,
    first_shift,
    second_gain,
    second_shift,
    attend_shrink,
    attend_expand,
    output_shrink,
    output_expand,
    upward_shrink,
    upward_expand,
    downward_shrink,
    downward_expand,
):
    i32 = jnp.int32
    col = lax.axis_index("col")
    row = lax.axis_index("row")
    stored = attend_shrink.shape[0]
    match = adapter_ids[:, None] == jnp.arange(adapter_place.shape[0], dtype=i32)[None, :]
    position = jnp.sum(jnp.where(match, adapter_place[None, :], 0), axis=1)
    meta = jnp.zeros((8, 128), i32)
    meta = meta.at[0, :REQ_COL].set(position).at[1, :REQ_COL].set(lengths)
    tok_all, meta_all = entry_gather(tokens.T, meta)
    widen_all = lax.all_gather(widen_weight, "col", axis=0, tiled=True)
    contract_all = lax.all_gather(contract_weight, "col", axis=0, tiled=True)
    tok_all = tok_all.reshape(64, SLOT, 256)

    requests = 64
    position = meta_all[:, 0, :REQ_COL].reshape(requests)
    length = meta_all[:, 1, :REQ_COL].reshape(requests)
    owner, local = position // stored, position % stored
    n = jnp.arange(requests, dtype=i32)
    same = (owner[None, :] == owner[:, None]) & (n[None, :] < n[:, None])
    rank = jnp.sum(same.astype(i32), axis=1)
    near = jnp.sum((same & (n[None, :] // REQ_COL == n[:, None] // REQ_COL)).astype(i32), axis=1)
    waves = (jnp.max(rank) + K) // K
    most = -(-32 // K)
    slots = jnp.arange(most * K, dtype=i32)
    mine = owner == col
    hit = mine[None, :] & (rank[None, :] == slots[:, None])
    req = jnp.sum(jnp.where(hit, n[None, :], 0), axis=1)
    loc = jnp.sum(jnp.where(hit, local[None, :], 0), axis=1)
    lens = jnp.maximum(jnp.sum(jnp.where(hit, length[None, :], 0), axis=1), 1)
    pair = jnp.arange(32, dtype=i32)
    out_hit = mine[None, :] & ((n // REQ_COL * 2 + near)[None, :] == pair[:, None])
    out_slot = jnp.sum(jnp.where(out_hit, rank[None, :], 0), axis=1)
    home_n = col * REQ_COL + jnp.arange(REQ_COL, dtype=i32)
    home_hit = home_n[:, None] == n[None, :]
    home_from = jnp.sum(jnp.where(home_hit, (owner * 2 + near)[None, :], 0), axis=1)
    row_id = row.astype(i32)[None]
    groups = K // GRP
    tall = K * SLOT
    gain1 = first_gain[None, :]
    shift1 = lax.dynamic_slice_in_dim(first_shift, row * 256, 256, 0)[None, :]
    gain2 = lax.dynamic_slice_in_dim(second_gain, row * 256, 256, 0)[None, :]
    shift2 = lax.dynamic_slice_in_dim(second_shift, row * 256, 256, 0)[None, :]

    def wave(w, weights):
        table = tuple(
            lax.dynamic_slice_in_dim(t, w * K, K, 0) for t in (req, loc, lens)
        ) + (row_id,)

        def shape(*dims, dtype=bf16):
            return jax.ShapeDtypeStruct(dims, dtype)

        def token_slot(i, g, req, loc, length, row):
            return (req[g * GRP + i], 0, 0)

        high = TOK + 3 * RANK
        low = TOK + RANK
        buf1 = staged(
            pack_kernel,
            "pack",
            table,
            pieces((1, SLOT, 256), token_slot) + by_slot((3 * RANK, 256)),
            own_group((1, high, 256)),
            shape(8, groups * high, 256),
            [tok_all] * GRP + [attend_shrink] * GRP,
        )
        if weights is None:
            buf1, qkv_all, out_all = wide_gather(
                buf1, attention_qkv_weight, attention_out_weight, 2
            )
            weights = (qkv_all.reshape(D, -1), out_all.reshape(D, -1))
        else:
            buf1 = row_gather(buf1, 6)
        qkv_all, out_all = weights
        buf2 = staged(
            attend_kernel,
            "attend",
            table,
            [by_group((8, high, 256)), whole((D, 768))]
            + by_slot((3, RANK, 256))
            + by_slot((RANK, 256)),
            own_group((1, low, 256)),
            shape(8, groups * low, 256),
            [buf1, qkv_all] + [attend_expand] * GRP + [output_shrink] * GRP,
        )
        buf2 = row_gather(buf2, 3)
        pre, stats = staged(
            mix_kernel,
            "mix",
            table,
            [by_group((8, low, 256)), own_group((1, high, 256)), whole((D, 256))]
            + by_slot((RANK, 256)),
            [rows_group(TOK, 256), rows_group(16, 256)],
            [shape(tall, 256, dtype=f32), shape(groups * 16, 256, dtype=f32)],
            [buf2, buf1, out_all] + [output_expand] * GRP,
        )
        stats = stat_gather(stats, 4)
        buf3 = staged(
            first_kernel,
            "first",
            table,
            [rows_group(TOK, 256), by_group((8, 16, 256)), whole((1, 256)), whole((1, 256))]
            + by_slot((RANK, 256)),
            own_group((1, low, 256)),
            shape(8, groups * low, 256),
            [pre, stats, gain1, shift1] + [upward_shrink] * GRP,
        )
        buf3 = row_gather(buf3, 3)
        part, ud = staged(
            hidden_kernel,
            "hidden",
            table,
            [by_group((8, low, 256)), whole((D, 1024)), whole((D, 1024))]
            + by_slot((RANK, 1024))
            + by_slot((RANK, 1024)),
            [
                pl.BlockSpec((4, 2, TOK, 256), lambda g, req, loc, length, row: (0, 0, g, 0)),
                own_group((1, RANK, 256)),
            ],
            [shape(4, 2, tall, 256), shape(8, groups * RANK, 256)],
            [buf3, widen_all, contract_all]
            + [upward_expand] * GRP
            + [downward_shrink] * GRP,
        )
        summed, ud = row_scatter(part, ud, 5)
        pre, stats = staged(
            second_kernel,
            "second",
            table,
            [by_group((4, TOK, 256)), by_group((8, RANK, 256)), own_group((1, low, 256))]
            + by_slot((RANK, 256)),
            [rows_group(TOK, 256), rows_group(16, 256)],
            [shape(tall, 256, dtype=f32), shape(groups * 16, 256, dtype=f32)],
            [summed, ud, buf3] + [downward_expand] * GRP,
        )
        stats = stat_gather(stats, 4)
        result = staged(
            last_kernel,
            "last",
            table,
            [rows_group(TOK, 256), by_group((8, 16, 256)), whole((1, 256)), whole((1, 256))],
            rows_group(TOK, 256),
            shape(tall, 256),
            [pre, stats, gain2, shift2],
        )
        return result, weights

    result, weights = wave(0, None)

    def quick(result):
        return jnp.take(result.reshape(K, SLOT, 256), jnp.minimum(out_slot, K - 1), axis=0)

    def longer(result):
        held = jnp.zeros((most, tall, 256), bf16)
        held = lax.dynamic_update_index_in_dim(held, result, 0, 0)
        held = lax.fori_loop(
            1, waves, lambda w, h: lax.dynamic_update_index_in_dim(h, wave(w, weights)[0], w, 0), held
        )
        return jnp.take(held.reshape(most * K, SLOT, 256), out_slot, axis=0)

    packed = lax.cond(waves > 1, longer, quick, result)
    return send_home(packed.reshape(16, 2, SLOT, 256), home_from).reshape(D, TOK)


def solution(mesh):
    return jax.shard_map(
        shards,
        mesh=mesh,
        in_specs=(
            P("row", "col"),
            P("col"),
            P("col"),
            P(),
            P("col", "row"),
            P("col", "row"),
            P("col", "row"),
            P("col", "row"),
            P("row"),
            P(),
            P(),
            P(),
            P("col", None, "row"),
            P("col", None, None, "row"),
            P("col", None, "row"),
            P("col", None, "row"),
            P("col", None, "row"),
            P("col", None, "row"),
            P("col", None, "row"),
            P("col", None, "row"),
        ),
        out_specs=P(None, "col"),
        check_vma=False,
    )
```

```python
import functools
import math

import jax
import jax.numpy as jnp
from jax import lax
from jax.experimental import pallas as pl
from jax.experimental.pallas import tpu as pltpu
from jax.sharding import PartitionSpec as P

D = 2048
HD = 128
SLOT = 64
RANK = 64
GRP = 4
TOK = GRP * SLOT
K = 12
REQ_COL = 4

eps = 1e-12
lowrank_scale = 0.5

MESH = pl.DeviceIdType.MESH
HBM = pl.BlockSpec(memory_space=pl.ANY)
NT = (((1,), (1,)), ((), ()))
f32 = jnp.float32
bf16 = jnp.bfloat16


def dot(a, b):
    return jnp.dot(a, b, preferred_element_type=f32)


def dot_nt(a, b):
    return lax.dot_general(a, b, NT, preferred_element_type=f32)


def greet(peers):
    barrier = pltpu.get_barrier_semaphore()
    for peer in peers:
        pl.semaphore_signal(barrier, inc=1, device_id=peer, device_id_type=MESH)
    pl.semaphore_wait(barrier, len(peers))


class Sender:
    def __init__(self, send_sem, recv_sem):
        self.send_sem, self.recv_sem = send_sem, recv_sem
        self.copies = []

    def start(self, src, dst, peer):
        i = len(self.copies)
        copy = pltpu.make_async_remote_copy(
            src_ref=src,
            dst_ref=dst,
            send_sem=self.send_sem.at[i],
            recv_sem=self.recv_sem.at[i],
            device_id=peer,
            device_id_type=MESH,
        )
        copy.start()
        self.copies.append(copy)
        return copy


def row_place():
    row = lax.axis_index("row")
    col = lax.axis_index("col")
    z, core = row // 2, row % 2
    return row, col, z, core


def ring_gather(buf, row, col, z, core, sender):
    half = buf.shape[1] // 2
    up, down = (z + 1) % 4, (z + 3) % 4
    far = (z + 2) % 4

    def part(zz, h):
        return buf.at[zz * 2 + core, pl.ds(h * half, half)]

    def dev(zz):
        return (zz * 2 + core, col)

    partner = (z * 2 + 1 - core, col)
    a0 = sender.start(part(z, 0), part(z, 0), dev(up))
    b1 = sender.start(part(z, 1), part(z, 1), dev(down))
    a1 = sender.start(part(z, 1), part(z, 1), dev(up))
    b0 = sender.start(part(z, 0), part(z, 0), dev(down))
    own = sender.start(buf.at[row], buf.at[row], partner)
    rest = [own]

    def across(zz, h):
        rest.append(sender.start(part(zz, h), part(zz, h), partner))

    yield
    a0.wait_recv()
    r0 = sender.start(part(down, 0), part(down, 0), dev(up))
    across(down, 0)
    b1.wait_recv()
    r1 = sender.start(part(up, 1), part(up, 1), dev(down))
    across(up, 1)
    yield
    a1.wait_recv()
    across(down, 1)
    b0.wait_recv()
    across(up, 0)
    yield
    r0.wait_recv()
    across(far, 0)
    r1.wait_recv()
    across(far, 1)
    yield
    for copy in rest:
        copy.wait_recv()


def finish(run):
    for _ in run:
        pass


def row_neighbours(col, z, core):
    return [
        (((z + 1) % 4) * 2 + core, col),
        (((z + 3) % 4) * 2 + core, col),
        (z * 2 + 1 - core, col),
    ]


def torus_gather(src, dst, row, x, y, sender):
    rows = src.shape[0]
    half, quarter = rows // 2, rows // 4

    def step(p, d):
        return (p + d) % 4

    flows = []
    for first in (0, 1):
        base = first * half

        def at(a, b, first=first):
            return (a * 4 + b) if first == 0 else (b * 4 + a)

        p, q = (x, y) if first == 0 else (y, x)

        def dev(a, b, at=at):
            return (row, at(a, b))

        def blk(a, b, lo, n, at=at, base=base):
            return dst.at[at(a, b), pl.ds(base + lo, n)]

        own = src.at[pl.ds(base, half)]
        flows.append((p, q, dev, blk, own))

    state = []
    for p, q, dev, blk, own in flows:
        here = blk(p, q, 0, half)
        a = sender.start(own, here, dev(step(p, 1), q))
        b = sender.start(own, here, dev(step(p, 3), q))
        c = sender.start(own, here, dev(p, step(q, 1)))
        d = sender.start(own, here, dev(p, step(q, 3)))
        state.append([a, b, [(p, c, d)]])
    yield
    relays = []
    for (p, q, dev, blk, own), st in zip(flows, state):
        a, b, second = st
        lo, hi = step(p, 3), step(p, 1)
        a.wait_recv()
        v = blk(lo, q, 0, quarter)
        r0 = sender.start(v, v, dev(step(p, 1), q))
        v = blk(lo, q, 0, half)
        second.append(
            (lo, sender.start(v, v, dev(p, step(q, 1))), sender.start(v, v, dev(p, step(q, 3))))
        )
        b.wait_recv()
        v = blk(hi, q, quarter, quarter)
        r1 = sender.start(v, v, dev(step(p, 3), q))
        v = blk(hi, q, 0, half)
        second.append(
            (hi, sender.start(v, v, dev(p, step(q, 1))), sender.start(v, v, dev(p, step(q, 3))))
        )
        st.append((r0, r1))
    yield
    for (p, q, dev, blk, own), st in zip(flows, state):
        second, (r0, r1) = st[2], st[3]
        r0.wait_recv()
        r1.wait_recv()
        fa = step(p, 2)
        v = blk(fa, q, 0, half)
        second.append(
            (fa, sender.start(v, v, dev(p, step(q, 1))), sender.start(v, v, dev(p, step(q, 3))))
        )
    yield
    last = []
    for i in range(4):
        for (p, q, dev, blk, own), st in zip(flows, state):
            pa, c, d = st[2][i]
            c.wait_recv()
            v = blk(pa, step(q, 3), 0, quarter)
            last.append(sender.start(v, v, dev(p, step(q, 1))))
            d.wait_recv()
            v = blk(pa, step(q, 1), quarter, quarter)
            last.append(sender.start(v, v, dev(p, step(q, 3))))
    yield
    for copy in last:
        copy.wait_recv()


def torus_neighbours(row, x, y):
    return [
        (row, (x + 1) % 4 * 4 + y),
        (row, (x + 3) % 4 * 4 + y),
        (row, x * 4 + (y + 1) % 4),
        (row, x * 4 + (y + 3) % 4),
    ]


def entry_kernel(
    tok_ref, meta_ref, tok_out, meta_out, tok_send, tok_recv, meta_send, meta_recv, own_sem
):
    row = lax.axis_index("row")
    col = lax.axis_index("col")
    x, y = col // 4, col % 4
    peers = [(row, (col + i) % 16) for i in range(1, 16)]
    own = [
        pltpu.make_async_copy(tok_ref, tok_out.at[col], own_sem.at[0]),
        pltpu.make_async_copy(meta_ref, meta_out.at[col], own_sem.at[1]),
    ]
    for copy in own:
        copy.start()
    greet(peers)
    tok_sender = Sender(tok_send, tok_recv)
    meta_sender = Sender(meta_send, meta_recv)
    run = torus_gather(tok_ref, tok_out, row, x, y, tok_sender)
    next(run)
    for peer in peers:
        meta_sender.start(meta_ref, meta_out.at[col], peer)
    finish(run)
    for copy in meta_sender.copies:
        copy.wait_recv()
    for sender in (tok_sender, meta_sender):
        for copy in sender.copies:
            copy.wait_send()
    for copy in own:
        copy.wait()


def entry_gather(tok, meta):
    arrays = (tok, meta)
    return pl.pallas_call(
        entry_kernel,
        out_shape=[jax.ShapeDtypeStruct((16,) + a.shape, a.dtype) for a in arrays],
        in_specs=[HBM] * 2,
        out_specs=[HBM] * 2,
        scratch_shapes=[pltpu.SemaphoreType.DMA((40,))] * 2
        + [pltpu.SemaphoreType.DMA((15,))] * 2
        + [pltpu.SemaphoreType.DMA((2,))],
        compiler_params=pltpu.CompilerParams(collective_id=0, has_side_effects=True),
        name="entry_gather",
    )(tok, meta)


def exit_kernel(pick, in_ref, out_ref, send_sem, recv_sem, r_send, r_recv, own_sem, arrived):
    row, col, z, core = row_place()
    peers = [(col + i) % 16 for i in range(1, 16)]
    here = arrived.at[pl.ds(col * 2, 2)]
    own = pltpu.make_async_copy(in_ref.at[col], here, own_sem)
    own.start()
    greet([(row, c) for c in peers] + row_neighbours(col, z, core))
    sender = Sender(send_sem, recv_sem)
    for c in peers:
        sender.start(in_ref.at[c], here, (row, c))
    own.wait()
    for copy in sender.copies:
        copy.wait_recv()
    mine = jnp.concatenate([arrived[pick[i]] for i in range(REQ_COL)], axis=0)
    out_ref[row] = mine.T
    r_sender = Sender(r_send, r_recv)
    finish(ring_gather(out_ref, row, col, z, core, r_sender))
    for copy in sender.copies + r_sender.copies:
        copy.wait_send()


def send_home(packed, pick):
    return pl.pallas_call(
        exit_kernel,
        out_shape=jax.ShapeDtypeStruct((8, 256, TOK), packed.dtype),
        in_specs=[pl.BlockSpec(memory_space=pltpu.SMEM), HBM],
        out_specs=pl.BlockSpec(memory_space=pltpu.VMEM),
        scratch_shapes=[
            pltpu.SemaphoreType.DMA((15,)),
            pltpu.SemaphoreType.DMA((15,)),
            pltpu.SemaphoreType.DMA((13,)),
            pltpu.SemaphoreType.DMA((13,)),
            pltpu.SemaphoreType.DMA,
            pltpu.VMEM((32, SLOT, 256), packed.dtype),
        ],
        compiler_params=pltpu.CompilerParams(collective_id=1, has_side_effects=True),
        name="send_home",
    )(pick, packed)


def scatter_sum(part, theirs, sums, row, col, z, core, sender):
    half = TOK // 2
    top, bottom = pl.ds(0, half), pl.ds(half, half)
    partner = (z * 2 + 1 - core, col)
    up, down = (((z + 1) % 4) * 2 + core, col), (((z + 3) % 4) * 2 + core, col)
    order = [(z + 2) % 4, (z + 1) % 4, (z + 3) % 4, z]
    swaps = [
        sender.start(part.at[zz, 1 - core], theirs.at[i], partner) for i, zz in enumerate(order)
    ]
    yield
    sent = []
    for i, zz in enumerate(order):
        swaps[i].wait_recv()
        both = (theirs[i].astype(f32) + part[zz, core].astype(f32)).astype(bf16)
        if i == 3:
            sums[3] = both
            continue
        theirs[i] = both
        if i == 0:
            r0 = sender.start(theirs.at[0, top], sums.at[4, top], up)
            r1 = sender.start(theirs.at[0, bottom], sums.at[4, bottom], down)
        else:
            sent.append(sender.start(theirs.at[i], sums.at[i], up if i == 1 else down))
    yield
    r0.wait_recv()
    sent.append(sender.start(sums.at[4, top], sums.at[0, top], up))
    r1.wait_recv()
    sent.append(sender.start(sums.at[4, bottom], sums.at[0, bottom], down))
    yield
    for copy in sent:
        copy.wait_recv()


def stat_exchange(stats, row, col, sender):
    copies = [
        sender.start(stats.at[row], stats.at[row], ((row + i) % 8, col)) for i in range(1, 8)
    ]
    yield
    for copy in copies:
        copy.wait_recv()


def slot_rows(i):
    return slice(i * SLOT, (i + 1) * SLOT)


def rank_sum(buf, first):
    total = buf[0, first : first + RANK, :].astype(f32)
    for r in range(1, 8):
        total = total + buf[r, first : first + RANK, :].astype(f32)
    return total.astype(bf16)


def weight_rows(weight, r):
    return weight[2 * r : 2 * r + 2].reshape(256, weight.shape[2])


def project(buf, weight):
    base = dot(buf[0, :TOK, :], weight_rows(weight, 0))
    for r in range(1, 8):
        base = base + dot(buf[r, :TOK, :], weight_rows(weight, r))
    return base


def gelu(v):
    return 0.5 * v * (1.0 + jnp.tanh(math.sqrt(2.0 / math.pi) * (v + 0.044715 * (v * v * v))))


def stats_of(values):
    lane = lax.broadcasted_iota(jnp.int32, (TOK, 128), 1)
    one = jnp.sum(values, axis=1, keepdims=True)
    two = jnp.sum(values * values, axis=1, keepdims=True)
    flipped = jnp.where(lane < 64, one, two).T
    return jnp.concatenate([flipped[0:8], flipped[64:72]], axis=0)


def norm_of(values, stats, gain, shift):
    total = stats[0]
    for r in range(1, 8):
        total = total + stats[r]
    total = total * (1.0 / D)
    mean = total[0:1, :]
    square = total[8:9, :]
    factor = lax.rsqrt(square - mean * mean + eps)
    both = jnp.concatenate(
        [
            jnp.broadcast_to(mean, (8, TOK)),
            jnp.broadcast_to(factor, (8, TOK)),
            jnp.zeros((112, TOK), f32),
        ],
        axis=0,
    ).T
    return (values - both[:, 0:1]) * both[:, 8:9] * gain + shift


GROUPS = K // GRP
HIGH = TOK + 3 * RANK
LOW = TOK + RANK
STORES = 8


def wave_kernel(*refs):
    table, vectors = refs[0], refs[1]
    tok_hbm = refs[2]
    weight_hbm = refs[3:7]
    store_hbm = refs[7 : 7 + STORES]
    out = refs[15]
    toks = refs[16]
    weights = refs[17:21]
    stores = refs[21 : 21 + STORES]
    buf1, buf2, buf3, bufu, part, theirs, sums, pre, stats = refs[29:38]
    load_sem, ring_send, ring_recv, torus_send, torus_recv = refs[38:43]
    swap_send, swap_recv, stat_send, stat_recv = refs[43:47]
    a_shrink, a_expand, o_shrink, o_expand, u_shrink, u_expand, d_shrink, d_expand = stores

    row, col, z, core = row_place()
    x, y = col // 4, col % 4
    loads = [pltpu.make_async_copy(tok_hbm, toks, load_sem.at[0])]
    for i in range(STORES):
        loads.append(pltpu.make_async_copy(store_hbm[i], stores[i], load_sem.at[1 + i]))
    for i in range(4):
        loads.append(
            pltpu.make_async_copy(weight_hbm[i], weights[i].at[col], load_sem.at[9 + i])
        )
    for copy in loads:
        copy.start()
    greet([((row + i) % 8, col) for i in range(1, 8)] + torus_neighbours(row, x, y))

    senders = []

    def sender(send, recv, i):
        senders.append(Sender(send.at[i], recv.at[i]))
        return senders[-1]

    def ring(buf, i):
        return ring_gather(buf, row, col, z, core, sender(ring_send, ring_recv, i))

    each = range(GROUPS)
    r1 = [ring(buf1.at[g], g) for g in each]
    r2 = [ring(buf2.at[g], GROUPS + g) for g in each]
    r3 = [ring(buf3.at[g], 2 * GROUPS + g) for g in each]
    ru = [ring(bufu.at[g], 3 * GROUPS + g) for g in each]
    tq, to, tw, tc = [
        torus_gather(weight_hbm[i], weights[i], row, x, y, sender(torus_send, torus_recv, i))
        for i in range(4)
    ]
    xs = [
        scatter_sum(
            part.at[g], theirs.at[g], sums.at[g], row, col, z, core,
            sender(swap_send, swap_recv, g),
        )
        for g in each
    ]
    s1 = [stat_exchange(stats.at[g], row, col, sender(stat_send, stat_recv, g)) for g in each]
    s2 = [
        stat_exchange(
            stats.at[GROUPS + g], row, col, sender(stat_send, stat_recv, GROUPS + g)
        )
        for g in each
    ]
    waited = set()

    def loaded(*which):
        for i in which:
            if i not in waited:
                waited.add(i)
                loads[i].wait()

    def go(*runs):
        for run in runs:
            next(run, None)

    first_slot = table[3, 0]

    def entry(kind, g, i):
        return table[kind, first_slot + (g * GRP + i)]

    def pack(g):
        loaded(0, 1)
        for i in range(GRP):
            v = toks[entry(0, g, i)]
            buf1[g, row, slot_rows(i), :] = v
            u = dot_nt(v, a_shrink[entry(1, g, i)]).astype(bf16)
            for j in range(3):
                buf1[g, row, TOK + j * RANK : TOK + (j + 1) * RANK, slot_rows(i)] = u[
                    :, j * RANK : (j + 1) * RANK
                ]

    def attend(g):
        loaded(2, 3, 9)
        buf = buf1.at[g]
        base = project(buf, weights[0])
        reduced = [rank_sum(buf, TOK + j * RANK) for j in range(3)]
        lane = lax.broadcasted_iota(jnp.int32, (SLOT, SLOT), 1)
        for i in range(GRP):
            at = entry(1, g, i)
            deltas = [
                dot(reduced[j][:, slot_rows(i)], a_expand[at, j]).astype(bf16).astype(f32)
                for j in range(3)
            ]
            valid = lane < entry(2, g, i)
            contexts = []
            for h in range(2):
                q, k, v = [
                    (
                        base[slot_rows(i), h * 384 + j * HD : h * 384 + (j + 1) * HD]
                        + lowrank_scale * deltas[j][:, h * HD : (h + 1) * HD]
                    ).astype(bf16)
                    for j in range(3)
                ]
                scores = dot_nt(q, k) / math.sqrt(HD)
                weight = jnp.where(valid, jnp.exp(scores), 0.0)
                probs = (weight / jnp.sum(weight, axis=1, keepdims=True)).astype(bf16)
                contexts.append(dot(probs, v).astype(bf16))
            context = jnp.concatenate(contexts, axis=1)
            buf2[g, row, slot_rows(i), :] = context
            buf2[g, row, TOK:LOW, slot_rows(i)] = dot_nt(context, o_shrink[at]).astype(bf16)

    def add_delta(g, reduced, expand, residual, base):
        for i in range(GRP):
            delta = dot(reduced[:, slot_rows(i)], expand[entry(1, g, i)])
            pre[g, slot_rows(i), :] = (
                residual[row, slot_rows(i), :].astype(f32)
                + base[slot_rows(i), :]
                + lowrank_scale * delta.astype(bf16).astype(f32)
            )

    def mix(g):
        loaded(4, 10)
        add_delta(g, rank_sum(buf2.at[g], TOK), o_expand, buf1.at[g], project(buf2.at[g], weights[1]))
        stats[g, row] = stats_of(pre[g])

    def first(g):
        loaded(5)
        v = norm_of(pre[g], stats.at[g], vectors[0:1], vectors[1:2]).astype(bf16)
        buf3[g, row, :TOK, :] = v
        for i in range(GRP):
            buf3[g, row, TOK:LOW, slot_rows(i)] = dot_nt(
                v[slot_rows(i), :], u_shrink[entry(1, g, i)]
            ).astype(bf16)

    def hidden(g):
        loaded(6, 7, 11, 12)
        base = project(buf3.at[g], weights[2])
        reduced = rank_sum(buf3.at[g], TOK)
        rows = []
        for i in range(GRP):
            at = entry(1, g, i)
            delta = dot(reduced[:, slot_rows(i)], u_expand[at]).astype(bf16).astype(f32)
            unit = gelu(base[slot_rows(i), :] + lowrank_scale * delta).astype(bf16)
            rows.append(unit)
            bufu[g, row, :, slot_rows(i)] = dot_nt(unit, d_shrink[at]).astype(bf16)
        units = jnp.concatenate(rows, axis=0)
        for r in range(8):
            part[g, r // 2, r % 2] = dot_nt(units, weight_rows(weights[3], r)).astype(bf16)

    def second(g):
        loaded(8)
        base = sums[g, 0].astype(f32)
        for r in range(1, 4):
            base = base + sums[g, r].astype(f32)
        add_delta(g, rank_sum(bufu.at[g], 0), d_expand, buf3.at[g], base)
        stats[GROUPS + g, row] = stats_of(pre[g])

    def last(g):
        v = norm_of(pre[g], stats.at[GROUPS + g], vectors[2:3], vectors[3:4])
        out[g * TOK : (g + 1) * TOK, :] = v.astype(bf16)

    go(tq)
    pack(0)
    go(r1[0])
    pack(1)
    go(tq, r1[0], r1[1])
    pack(2)
    go(tq, r1[0], r1[1], r1[0], r1[2], tq, to, r1[1], r1[0], tq)
    attend(0)
    go(r2[0], to, to, tw, r1[1], r1[2], r1[2], r2[0], r1[1])
    attend(1)
    go(r2[1], to, tw, r1[2], r2[0], r1[2])
    attend(2)
    go(r2[2], r2[0], r2[1], tw, tc, to, r2[1], r2[0])
    mix(0)
    go(s1[0], r2[1], r2[2], r2[2], tw, tc, r2[1])
    mix(1)
    go(s1[1], s1[0])
    first(0)
    go(r3[0], r2[2], tc, r2[2])
    mix(2)
    go(s1[2], s1[1])
    first(1)
    go(r3[0], r3[1], s1[2])
    first(2)
    go(tc, r3[0], r3[1], r3[0], r3[2], r3[1], r3[0], tw, tc)
    hidden(0)
    go(xs[0], ru[0], r3[1], r3[2], r3[2], r3[1])
    hidden(1)
    go(xs[1], ru[1], xs[0], ru[0], r3[2], r3[2], xs[0])
    hidden(2)
    go(xs[2], ru[2], xs[1], ru[1], xs[0], ru[0], ru[0], ru[0], xs[1], xs[2], ru[2])
    second(0)
    go(s2[0], ru[1], ru[1], xs[2], xs[1], ru[1])
    second(1)
    go(s2[1], s2[0])
    last(0)
    go(ru[2], ru[2], xs[2], ru[2])
    second(2)
    go(s2[2], s2[1])
    last(1)
    go(s2[2])
    last(2)
    for run in r1 + r2 + r3 + ru + [tq, to, tw, tc] + xs + s1 + s2:
        assert next(run, row) is row
    for one in senders:
        for copy in one.copies:
            copy.wait_send()


def run_wave(table, vectors, toks, base_weights, stores):
    vmem = pl.BlockSpec(memory_space=pltpu.VMEM)
    dma = pltpu.SemaphoreType.DMA
    rings = 4 * GROUPS
    return pl.pallas_call(
        wave_kernel,
        out_shape=jax.ShapeDtypeStruct((K * SLOT, 256), bf16),
        in_specs=[pl.BlockSpec(memory_space=pltpu.SMEM), vmem] + [HBM] * 13,
        out_specs=vmem,
        scratch_shapes=[pltpu.VMEM(toks.shape, bf16)]
        + [pltpu.VMEM((16,) + w.shape, bf16) for w in base_weights]
        + [pltpu.VMEM(s.shape, bf16) for s in stores]
        + [
            pltpu.VMEM((GROUPS, 8, HIGH, 256), bf16),
            pltpu.VMEM((GROUPS, 8, LOW, 256), bf16),
            pltpu.VMEM((GROUPS, 8, LOW, 256), bf16),
            pltpu.VMEM((GROUPS, 8, RANK, 256), bf16),
            pltpu.VMEM((GROUPS, 4, 2, TOK, 256), bf16),
            pltpu.VMEM((GROUPS, 4, TOK, 256), bf16),
            pltpu.VMEM((GROUPS, 5, TOK, 256), bf16),
            pltpu.VMEM((GROUPS, TOK, 256), f32),
            pltpu.VMEM((2 * GROUPS, 8, 16, 256), f32),
        ]
        + [dma((13,)), dma((rings, 13)), dma((rings, 13)), dma((4, 40)), dma((4, 40))]
        + [dma((GROUPS, 10)), dma((GROUPS, 10)), dma((2 * GROUPS, 7)), dma((2 * GROUPS, 7))],
        compiler_params=pltpu.CompilerParams(
            collective_id=2, has_side_effects=True, vmem_limit_bytes=67043328
        ),
        name="wave",
    )(table, vectors, toks, *base_weights, *stores)


def shards(
    tokens,
    lengths,
    adapter_ids,
    adapter_place,
    attention_qkv_weight,
    attention_out_weight,
    widen_weight,
    contract_weight,
    first_gain,
    first_shift,
    second_gain,
    second_shift,
    *stores,
):
    i32 = jnp.int32
    col = lax.axis_index("col")
    row = lax.axis_index("row")
    stored = stores[0].shape[0]
    match = adapter_ids[:, None] == jnp.arange(adapter_place.shape[0], dtype=i32)[None, :]
    position = jnp.sum(jnp.where(match, adapter_place[None, :], 0), axis=1)
    meta = jnp.zeros((8, 128), i32)
    meta = meta.at[0, :REQ_COL].set(position).at[1, :REQ_COL].set(lengths)
    tok_all, meta_all = entry_gather(tokens.T, meta)
    tok_all = tok_all.reshape(64, SLOT, 256)

    requests = 64
    position = meta_all[:, 0, :REQ_COL].reshape(requests)
    length = meta_all[:, 1, :REQ_COL].reshape(requests)
    owner, local = position // stored, position % stored
    n = jnp.arange(requests, dtype=i32)
    same = (owner[None, :] == owner[:, None]) & (n[None, :] < n[:, None])
    rank = jnp.sum(same.astype(i32), axis=1)
    near = jnp.sum((same & (n[None, :] // REQ_COL == n[:, None] // REQ_COL)).astype(i32), axis=1)
    waves = (jnp.max(rank) + K) // K
    most = -(-32 // K)
    slots = jnp.arange(most * K, dtype=i32)
    mine = owner == col
    hit = mine[None, :] & (rank[None, :] == slots[:, None])
    facts = jnp.stack([n, local, length - 1])
    table = jnp.sum(jnp.where(hit[None], facts[:, None, :], 0), axis=2)
    table = table + jnp.array([[0], [0], [1]], i32)
    pair = jnp.arange(32, dtype=i32)
    out_hit = mine[None, :] & ((n // REQ_COL * 2 + near)[None, :] == pair[:, None])
    out_slot = jnp.sum(jnp.where(out_hit, rank[None, :], 0), axis=1)
    home_n = col * REQ_COL + jnp.arange(REQ_COL, dtype=i32)
    home_hit = home_n[:, None] == n[None, :]
    home_from = jnp.sum(jnp.where(home_hit, (owner * 2 + near)[None, :], 0), axis=1)
    tail = [lax.dynamic_slice_in_dim(v, row * 256, 256, 0) for v in (first_shift, second_gain, second_shift)]
    vectors = jnp.stack([first_gain] + tail)
    base_weights = (attention_qkv_weight, attention_out_weight, widen_weight, contract_weight)

    def wave(w, held):
        with_start = jnp.concatenate([table, jnp.full((1, most * K), w * K, i32)])
        result = run_wave(with_start, vectors, tok_all, base_weights, stores)
        return lax.dynamic_update_index_in_dim(held, result, w, 0)

    held = lax.fori_loop(0, waves, wave, jnp.zeros((most, K * SLOT, 256), bf16))
    packed = jnp.take(held.reshape(most * K, SLOT, 256), out_slot, axis=0)
    return send_home(packed.reshape(16, 2, SLOT, 256), home_from).reshape(D, TOK)


def solution(mesh):
    return jax.shard_map(
        shards,
        mesh=mesh,
        in_specs=(
            P("row", "col"),
            P("col"),
            P("col"),
            P(),
            P("col", "row"),
            P("col", "row"),
            P("col", "row"),
            P("col", "row"),
            P("row"),
            P(),
            P(),
            P(),
            P("col", None, "row"),
            P("col", None, None, "row"),
            P("col", None, "row"),
            P("col", None, "row"),
            P("col", None, "row"),
            P("col", None, "row"),
            P("col", None, "row"),
            P("col", None, "row"),
        ),
        out_specs=P(None, "col"),
        check_vma=False,
    )
```

```python
import functools
import math

import jax
import jax.numpy as jnp
from jax import lax
from jax.experimental import pallas as pl
from jax.experimental.pallas import tpu as pltpu
from jax.sharding import PartitionSpec as P

D = 2048
HD = 128
SLOT = 64
RANK = 64
GRP = 4
TOK = GRP * SLOT
K = 12
REQ_COL = 4

eps = 1e-12
lowrank_scale = 0.5

MESH = pl.DeviceIdType.MESH
HBM = pl.BlockSpec(memory_space=pl.ANY)
NT = (((1,), (1,)), ((), ()))
f32 = jnp.float32
bf16 = jnp.bfloat16


def dot(a, b):
    return jnp.dot(a, b, preferred_element_type=f32)


def dot_nt(a, b):
    return lax.dot_general(a, b, NT, preferred_element_type=f32)


def greet(peers):
    barrier = pltpu.get_barrier_semaphore()
    for peer in peers:
        pl.semaphore_signal(barrier, inc=1, device_id=peer, device_id_type=MESH)
    pl.semaphore_wait(barrier, len(peers))


class Sender:
    def __init__(self, send_sem, recv_sem):
        self.send_sem, self.recv_sem = send_sem, recv_sem
        self.copies = []

    def start(self, src, dst, peer):
        i = len(self.copies)
        copy = pltpu.make_async_remote_copy(
            src_ref=src,
            dst_ref=dst,
            send_sem=self.send_sem.at[i],
            recv_sem=self.recv_sem.at[i],
            device_id=peer,
            device_id_type=MESH,
        )
        copy.start()
        self.copies.append(copy)
        return copy


def row_place():
    row = lax.axis_index("row")
    col = lax.axis_index("col")
    z, core = row // 2, row % 2
    return row, col, z, core


def ring_gather(buf, row, col, z, core, sender):
    half = buf.shape[1] // 2
    up, down = (z + 1) % 4, (z + 3) % 4
    far = (z + 2) % 4

    def part(zz, h):
        return buf.at[zz * 2 + core, pl.ds(h * half, half)]

    def dev(zz):
        return (zz * 2 + core, col)

    partner = (z * 2 + 1 - core, col)
    a0 = sender.start(part(z, 0), part(z, 0), dev(up))
    b1 = sender.start(part(z, 1), part(z, 1), dev(down))
    a1 = sender.start(part(z, 1), part(z, 1), dev(up))
    b0 = sender.start(part(z, 0), part(z, 0), dev(down))
    own = sender.start(buf.at[row], buf.at[row], partner)
    rest = [own]

    def across(zz, h):
        rest.append(sender.start(part(zz, h), part(zz, h), partner))

    yield
    a0.wait_recv()
    r0 = sender.start(part(down, 0), part(down, 0), dev(up))
    across(down, 0)
    b1.wait_recv()
    r1 = sender.start(part(up, 1), part(up, 1), dev(down))
    across(up, 1)
    yield
    a1.wait_recv()
    across(down, 1)
    b0.wait_recv()
    across(up, 0)
    yield
    r0.wait_recv()
    across(far, 0)
    r1.wait_recv()
    across(far, 1)
    yield
    for copy in rest:
        copy.wait_recv()


def finish(run):
    for _ in run:
        pass


def row_neighbours(col, z, core):
    return [
        (((z + 1) % 4) * 2 + core, col),
        (((z + 3) % 4) * 2 + core, col),
        (z * 2 + 1 - core, col),
    ]


def torus_gather(src, dst, row, x, y, sender):
    rows = src.shape[0]
    half, quarter = rows // 2, rows // 4

    def step(p, d):
        return (p + d) % 4

    flows = []
    for first in (0, 1):
        base = first * half

        def at(a, b, first=first):
            return (a * 4 + b) if first == 0 else (b * 4 + a)

        p, q = (x, y) if first == 0 else (y, x)

        def dev(a, b, at=at):
            return (row, at(a, b))

        def blk(a, b, lo, n, at=at, base=base):
            return dst.at[at(a, b), pl.ds(base + lo, n)]

        own = src.at[pl.ds(base, half)]
        flows.append((p, q, dev, blk, own))

    state = []
    for p, q, dev, blk, own in flows:
        here = blk(p, q, 0, half)
        a = sender.start(own, here, dev(step(p, 1), q))
        b = sender.start(own, here, dev(step(p, 3), q))
        c = sender.start(own, here, dev(p, step(q, 1)))
        d = sender.start(own, here, dev(p, step(q, 3)))
        state.append([a, b, [(p, c, d)]])
    yield
    relays = []
    for (p, q, dev, blk, own), st in zip(flows, state):
        a, b, second = st
        lo, hi = step(p, 3), step(p, 1)
        a.wait_recv()
        v = blk(lo, q, 0, quarter)
        r0 = sender.start(v, v, dev(step(p, 1), q))
        v = blk(lo, q, 0, half)
        second.append(
            (lo, sender.start(v, v, dev(p, step(q, 1))), sender.start(v, v, dev(p, step(q, 3))))
        )
        b.wait_recv()
        v = blk(hi, q, quarter, quarter)
        r1 = sender.start(v, v, dev(step(p, 3), q))
        v = blk(hi, q, 0, half)
        second.append(
            (hi, sender.start(v, v, dev(p, step(q, 1))), sender.start(v, v, dev(p, step(q, 3))))
        )
        st.append((r0, r1))
    yield
    for (p, q, dev, blk, own), st in zip(flows, state):
        second, (r0, r1) = st[2], st[3]
        r0.wait_recv()
        r1.wait_recv()
        fa = step(p, 2)
        v = blk(fa, q, 0, half)
        second.append(
            (fa, sender.start(v, v, dev(p, step(q, 1))), sender.start(v, v, dev(p, step(q, 3))))
        )
    yield
    last = []
    for i in range(4):
        for (p, q, dev, blk, own), st in zip(flows, state):
            pa, c, d = st[2][i]
            c.wait_recv()
            v = blk(pa, step(q, 3), 0, quarter)
            last.append(sender.start(v, v, dev(p, step(q, 1))))
            d.wait_recv()
            v = blk(pa, step(q, 1), quarter, quarter)
            last.append(sender.start(v, v, dev(p, step(q, 3))))
    yield
    for copy in last:
        copy.wait_recv()


def torus_neighbours(row, x, y):
    return [
        (row, (x + 1) % 4 * 4 + y),
        (row, (x + 3) % 4 * 4 + y),
        (row, x * 4 + (y + 1) % 4),
        (row, x * 4 + (y + 3) % 4),
    ]


def entry_kernel(
    tok_ref, meta_ref, tok_out, meta_out, tok_send, tok_recv, meta_send, meta_recv, own_sem
):
    row = lax.axis_index("row")
    col = lax.axis_index("col")
    x, y = col // 4, col % 4
    peers = [(row, (col + i) % 16) for i in range(1, 16)]
    own = [
        pltpu.make_async_copy(tok_ref, tok_out.at[col], own_sem.at[0]),
        pltpu.make_async_copy(meta_ref, meta_out.at[col], own_sem.at[1]),
    ]
    for copy in own:
        copy.start()
    greet(peers)
    tok_sender = Sender(tok_send, tok_recv)
    meta_sender = Sender(meta_send, meta_recv)
    run = torus_gather(tok_ref, tok_out, row, x, y, tok_sender)
    next(run)
    for peer in peers:
        meta_sender.start(meta_ref, meta_out.at[col], peer)
    finish(run)
    for copy in meta_sender.copies:
        copy.wait_recv()
    for sender in (tok_sender, meta_sender):
        for copy in sender.copies:
            copy.wait_send()
    for copy in own:
        copy.wait()


def entry_gather(tok, meta):
    arrays = (tok, meta)
    return pl.pallas_call(
        entry_kernel,
        out_shape=[jax.ShapeDtypeStruct((16,) + a.shape, a.dtype) for a in arrays],
        in_specs=[HBM] * 2,
        out_specs=[HBM] * 2,
        scratch_shapes=[pltpu.SemaphoreType.DMA((40,))] * 2
        + [pltpu.SemaphoreType.DMA((15,))] * 2
        + [pltpu.SemaphoreType.DMA((2,))],
        compiler_params=pltpu.CompilerParams(collective_id=0, has_side_effects=True),
        name="entry_gather",
    )(tok, meta)


def scatter_sum(part, theirs, sums, row, col, z, core, sender):
    half = TOK // 2
    top, bottom = pl.ds(0, half), pl.ds(half, half)
    partner = (z * 2 + 1 - core, col)
    up, down = (((z + 1) % 4) * 2 + core, col), (((z + 3) % 4) * 2 + core, col)
    order = [(z + 2) % 4, (z + 1) % 4, (z + 3) % 4, z]
    swaps = [
        sender.start(part.at[zz, 1 - core], theirs.at[i], partner) for i, zz in enumerate(order)
    ]
    yield
    far, sent = [], []
    for i, zz in enumerate(order):
        swaps[i].wait_recv()
        both = (theirs[i].astype(f32) + part[zz, core].astype(f32)).astype(bf16)
        if i == 3:
            sums[3] = both
            continue
        theirs[i] = both
        if i == 0:
            far.append(sender.start(theirs.at[0, top], sums.at[0, top], up))
            far.append(sender.start(theirs.at[0, bottom], sums.at[0, bottom], down))
        elif i == 1:
            sent.append(sender.start(theirs.at[1, bottom], sums.at[1, bottom], up))
        else:
            sent.append(sender.start(theirs.at[2, top], sums.at[2, top], down))
    yield
    for i, rows, peer in ((1, top, up), (2, bottom, down)):
        far[i - 1].wait_recv()
        merged = theirs[i, rows].astype(f32) + sums[0, rows].astype(f32)
        theirs[i, rows] = merged.astype(bf16)
        sent.append(sender.start(theirs.at[i, rows], sums.at[i, rows], peer))
    yield
    for copy in sent:
        copy.wait_recv()


def stat_exchange(stats, row, col, sender):
    copies = [
        sender.start(stats.at[row], stats.at[row], ((row + i) % 8, col)) for i in range(1, 8)
    ]
    yield
    for copy in copies:
        copy.wait_recv()


def slot_rows(i):
    return slice(i * SLOT, (i + 1) * SLOT)


def rank_sum(buf, first):
    total = buf[0, first : first + RANK, :].astype(f32)
    for r in range(1, 8):
        total = total + buf[r, first : first + RANK, :].astype(f32)
    return total.astype(bf16)


def weight_rows(weight, r):
    return weight[2 * r : 2 * r + 2].reshape(256, weight.shape[2])


def project(buf, weight):
    base = dot(buf[0, :TOK, :], weight_rows(weight, 0))
    for r in range(1, 8):
        base = base + dot(buf[r, :TOK, :], weight_rows(weight, r))
    return base


def gelu(v):
    return 0.5 * v * (1.0 + jnp.tanh(math.sqrt(2.0 / math.pi) * (v + 0.044715 * (v * v * v))))


def stats_of(values):
    lane = lax.broadcasted_iota(jnp.int32, (TOK, 128), 1)
    one = jnp.sum(values, axis=1, keepdims=True)
    two = jnp.sum(values * values, axis=1, keepdims=True)
    flipped = jnp.where(lane < 64, one, two).T
    return jnp.concatenate([flipped[0:8], flipped[64:72]], axis=0)


def norm_of(values, stats, gain, shift):
    total = stats[0]
    for r in range(1, 8):
        total = total + stats[r]
    total = total * (1.0 / D)
    mean = total[0:1, :]
    square = total[8:9, :]
    factor = lax.rsqrt(square - mean * mean + eps)
    both = jnp.concatenate(
        [
            jnp.broadcast_to(mean, (8, TOK)),
            jnp.broadcast_to(factor, (8, TOK)),
            jnp.zeros((112, TOK), f32),
        ],
        axis=0,
    ).T
    return (values - both[:, 0:1]) * both[:, 8:9] * gain + shift


HIGH = TOK + 3 * RANK
LOW = TOK + RANK
STORES = 8


def wave_kernel(groups, *refs):
    start, table = refs[0], refs[1]
    gain1, shift1, gain2, shift2 = refs[2:6]
    out_hbm, tok_hbm = refs[6], refs[7]
    weight_hbm = refs[8:12]
    store_hbm = refs[12 : 12 + STORES]
    out = refs[20]
    toks = refs[21]
    weights = refs[22:26]
    stores = refs[26 : 26 + STORES]
    buf1, buf2, buf3, bufu, part, theirs, sums, pre, stats = refs[34:43]
    result, packed, arrived, held = refs[43:47]
    load_sem, ring_send, ring_recv, torus_send, torus_recv = refs[47:52]
    swap_send, swap_recv, stat_send, stat_recv, exit_send, exit_recv = refs[52:58]
    a_shrink, a_expand, o_shrink, o_expand, u_shrink, u_expand, d_shrink, d_expand = stores
    slots = groups * GRP

    row, col, z, core = row_place()
    x, y = col // 4, col % 4
    loads = [pltpu.make_async_copy(tok_hbm, toks, load_sem.at[0])]
    for i in range(STORES):
        loads.append(pltpu.make_async_copy(store_hbm[i], stores[i], load_sem.at[1 + i]))
    for i in range(4):
        loads.append(
            pltpu.make_async_copy(weight_hbm[i], weights[i].at[col], load_sem.at[9 + i])
        )
    loads.append(pltpu.make_async_copy(out.at[row], held, load_sem.at[13]))
    columns = [(col + i) % 16 for i in range(1, 16)]

    def begin(*which):
        for i in which:
            loads[i].start()

    begin(0, 1, 9)
    greet([((row + i) % 8, col) for i in range(1, 8)] + [(row, c) for c in columns])

    senders = []

    def sender(send, recv, i):
        senders.append(Sender(send.at[i], recv.at[i]))
        return senders[-1]

    def ring(buf, i):
        return ring_gather(buf, row, col, z, core, sender(ring_send, ring_recv, i))

    each = range(groups)
    r1 = [ring(buf1.at[g], g) for g in each]
    r2 = [ring(buf2.at[g], groups + g) for g in each]
    r3 = [ring(buf3.at[g], 2 * groups + g) for g in each]
    ru = [ring(bufu.at[g], 3 * groups + g) for g in each]
    rx = ring(out, 4 * groups)
    tq, to, tw, tc = [
        torus_gather(weight_hbm[i], weights[i], row, x, y, sender(torus_send, torus_recv, i))
        for i in range(4)
    ]
    xs = [
        scatter_sum(
            part.at[g], theirs.at[g], sums.at[g], row, col, z, core,
            sender(swap_send, swap_recv, g),
        )
        for g in each
    ]
    s1 = [stat_exchange(stats.at[g], row, col, sender(stat_send, stat_recv, g)) for g in each]
    s2 = [
        stat_exchange(
            stats.at[groups + g], row, col, sender(stat_send, stat_recv, groups + g)
        )
        for g in each
    ]
    waited = set()

    def loaded(*which):
        for i in which:
            if i not in waited:
                waited.add(i)
                loads[i].wait()

    first_slot = start[0]

    def entry(kind, g, i):
        return table[kind, first_slot + (g * GRP + i)]

    def own_features(ref):
        return ref[:, pl.ds(pl.multiple_of(row * 256, 256), 256)]

    def pack(g):
        loaded(0, 1)
        for i in range(GRP):
            v = toks[entry(0, g, i)]
            buf1[g, row, slot_rows(i), :] = v
            u = dot_nt(v, a_shrink[entry(1, g, i)]).astype(bf16)
            for j in range(3):
                buf1[g, row, TOK + j * RANK : TOK + (j + 1) * RANK, slot_rows(i)] = u[
                    :, j * RANK : (j + 1) * RANK
                ]

    def attend(g):
        loaded(2, 3, 9)
        buf = buf1.at[g]
        base = project(buf, weights[0])
        reduced = [rank_sum(buf, TOK + j * RANK) for j in range(3)]
        lane = lax.broadcasted_iota(jnp.int32, (SLOT, SLOT), 1)
        for i in range(GRP):
            at = entry(1, g, i)
            deltas = [
                dot(reduced[j][:, slot_rows(i)], a_expand[at, j]).astype(bf16).astype(f32)
                for j in range(3)
            ]
            valid = lane < entry(2, g, i)
            contexts = []
            for h in range(2):
                q, k, v = [
                    (
                        base[slot_rows(i), h * 384 + j * HD : h * 384 + (j + 1) * HD]
                        + lowrank_scale * deltas[j][:, h * HD : (h + 1) * HD]
                    ).astype(bf16)
                    for j in range(3)
                ]
                scores = dot_nt(q, k) / math.sqrt(HD)
                weight = jnp.where(valid, jnp.exp(scores), 0.0)
                probs = (weight / jnp.sum(weight, axis=1, keepdims=True)).astype(bf16)
                contexts.append(dot(probs, v).astype(bf16))
            context = jnp.concatenate(contexts, axis=1)
            buf2[g, row, slot_rows(i), :] = context
            buf2[g, row, TOK:LOW, slot_rows(i)] = dot_nt(context, o_shrink[at]).astype(bf16)

    def add_delta(g, reduced, expand, residual, base):
        for i in range(GRP):
            delta = dot(reduced[:, slot_rows(i)], expand[entry(1, g, i)])
            pre[g, slot_rows(i), :] = (
                residual[row, slot_rows(i), :].astype(f32)
                + base[slot_rows(i), :]
                + lowrank_scale * delta.astype(bf16).astype(f32)
            )

    def mix(g):
        loaded(4, 10)
        add_delta(g, rank_sum(buf2.at[g], TOK), o_expand, buf1.at[g], project(buf2.at[g], weights[1]))
        stats[g, row] = stats_of(pre[g])

    def first(g):
        loaded(5)
        v = norm_of(pre[g], stats.at[g], gain1[...], own_features(shift1)).astype(bf16)
        buf3[g, row, :TOK, :] = v
        for i in range(GRP):
            buf3[g, row, TOK:LOW, slot_rows(i)] = dot_nt(
                v[slot_rows(i), :], u_shrink[entry(1, g, i)]
            ).astype(bf16)

    units = {}

    def rise(g):
        loaded(6, 7, 11)
        base = project(buf3.at[g], weights[2])
        reduced = rank_sum(buf3.at[g], TOK)
        rows = []
        for i in range(GRP):
            at = entry(1, g, i)
            delta = dot(reduced[:, slot_rows(i)], u_expand[at]).astype(bf16).astype(f32)
            unit = gelu(base[slot_rows(i), :] + lowrank_scale * delta).astype(bf16)
            rows.append(unit)
            bufu[g, row, :, slot_rows(i)] = dot_nt(unit, d_shrink[at]).astype(bf16)
        units[g] = jnp.concatenate(rows, axis=0)

    def fall(g):
        loaded(12)
        for r in range(8):
            part[g, r // 2, r % 2] = dot_nt(units[g], weight_rows(weights[3], r)).astype(bf16)

    def second(g):
        loaded(8)
        base = sums[g, 1].astype(f32) + sums[g, 2].astype(f32) + sums[g, 3].astype(f32)
        add_delta(g, rank_sum(bufu.at[g], 0), d_expand, buf3.at[g], base)
        stats[groups + g, row] = stats_of(pre[g])

    def last(g):
        v = norm_of(
            pre[g], stats.at[groups + g], own_features(gain2), own_features(shift2)
        ).astype(bf16)
        for i in range(GRP):
            result[g * GRP + i] = v[slot_rows(i), :]

    def leave():
        @pl.loop(0, 32)
        def _(p):
            slot = table[3, p] - first_slot
            packed[p] = result[jnp.minimum(jnp.maximum(slot, 0), slots - 1)]

        one = Sender(exit_send, exit_recv)
        senders.append(one)
        here = pl.ds(col * 2, 2)
        for c in columns:
            one.start(packed.at[pl.ds(c * 2, 2)], arrived.at[here], (row, c))
        arrived[here] = packed[here]
        loaded(13)
        lane = lax.broadcasted_iota(jnp.int32, (256, TOK), 1)
        fresh = jnp.zeros((256, TOK), jnp.int32)
        for i in range(REQ_COL):
            slot = table[5, i] - first_slot
            now = jnp.where((slot >= 0) & (slot < slots), 1, 0)
            fresh = jnp.where(lane // SLOT == i, now, fresh)
        for copy in one.copies:
            copy.wait_recv()
        mine = jnp.concatenate([arrived[table[4, i]] for i in range(REQ_COL)], axis=0)
        flipped = mine.astype(f32).T
        held[...] = jnp.where(fresh == 1, flipped, held[...].astype(f32)).astype(bf16)
        store = pltpu.make_async_copy(held, out.at[row], load_sem.at[14])
        store.start()
        store.wait()

    def go(*items):
        for item in items:
            if isinstance(item, tuple):
                what, g = item
                if g >= groups:
                    continue
                if callable(what):
                    what(g)
                    continue
                item = what[g]
            next(item, None)

    go(tq, (pack, 0))
    begin(*range(2, 9), 10, 11, 12, 13)
    go((r1, 0), (pack, 1), tq, (r1, 0), (r1, 1), (pack, 2), tq, (r1, 0), (r1, 1), (r1, 0), (r1, 2))
    go(tq, to, tw, (r1, 1), (r1, 0), tq, (attend, 0))
    go((r2, 0), to, to, tw, (r1, 1), (r1, 2), (r1, 2), (r2, 0), (r1, 1), tc, (attend, 1))
    go((r2, 1), to, tw, (r1, 2), (r2, 0), (r1, 2), (attend, 2))
    go((r2, 2), (r2, 0), (r2, 1), tw, tc, to, (r2, 1), (r2, 0), (mix, 0))
    go((s1, 0), (r2, 1), (r2, 2), (r2, 2), tc, (r2, 1), (mix, 1), (s1, 1), (s1, 0), (first, 0))
    go((r3, 0), (r2, 2), tc, (r2, 2), (mix, 2), (s1, 2), (s1, 1), (first, 1))
    go((r3, 0), (r3, 1), (s1, 2), (first, 2))
    go((r3, 0), (r3, 1), (r3, 0), (r3, 2), (r3, 1), (r3, 0), tw, (rise, 0), tc, (fall, 0))
    go((xs, 0), (ru, 0), (r3, 1), (r3, 2), (r3, 2), (r3, 1), (rise, 1), (fall, 1))
    go((xs, 1), (ru, 1), (xs, 0), (ru, 0), (r3, 2), (r3, 2), (xs, 0), (rise, 2), (fall, 2))
    go((xs, 2), (ru, 2), (xs, 1), (ru, 1), (xs, 0), (ru, 0), (ru, 0), (ru, 0), (xs, 1))
    go((xs, 2), (ru, 2), (second, 0), (s2, 0), (ru, 1), (ru, 1), (xs, 2), (xs, 1), (ru, 1))
    go((second, 1), (s2, 1), (s2, 0), (last, 0), (ru, 2), (ru, 2), (xs, 2), (ru, 2))
    go((second, 2), (s2, 2), (s2, 1), (last, 1), (s2, 2), (last, 2))
    leave()
    finish(rx)
    for run in r1 + r2 + r3 + ru + [rx, tq, to, tw, tc] + xs + s1 + s2:
        assert next(run, row) is row
    for one in senders:
        for copy in one.copies:
            copy.wait_send()


def run_wave(groups, start, table, vectors, out, toks, base_weights, stores):
    smem = pl.BlockSpec(memory_space=pltpu.SMEM)
    vmem = pl.BlockSpec(memory_space=pltpu.VMEM)
    dma = pltpu.SemaphoreType.DMA
    rings = 4 * groups + 1
    return pl.pallas_call(
        functools.partial(wave_kernel, groups),
        out_shape=jax.ShapeDtypeStruct(out.shape, out.dtype),
        in_specs=[smem] * 2 + [vmem] * 4 + [HBM] * 14,
        out_specs=HBM,
        scratch_shapes=[pltpu.VMEM(toks.shape, bf16)]
        + [pltpu.VMEM((16,) + w.shape, bf16) for w in base_weights]
        + [pltpu.VMEM(s.shape, bf16) for s in stores]
        + [
            pltpu.VMEM((groups, 8, HIGH, 256), bf16),
            pltpu.VMEM((groups, 8, LOW, 256), bf16),
            pltpu.VMEM((groups, 8, LOW, 256), bf16),
            pltpu.VMEM((groups, 8, RANK, 256), bf16),
            pltpu.VMEM((groups, 4, 2, TOK, 256), bf16),
            pltpu.VMEM((groups, 4, TOK, 256), bf16),
            pltpu.VMEM((groups, 4, TOK, 256), bf16),
            pltpu.VMEM((groups, TOK, 256), f32),
            pltpu.VMEM((2 * groups, 8, 16, 256), f32),
            pltpu.VMEM((groups * GRP, SLOT, 256), bf16),
            pltpu.VMEM((32, SLOT, 256), bf16),
            pltpu.VMEM((32, SLOT, 256), bf16),
            pltpu.VMEM((256, TOK), bf16),
        ]
        + [dma((15,)), dma((rings, 13)), dma((rings, 13)), dma((4, 40)), dma((4, 40))]
        + [dma((groups, 10)), dma((groups, 10)), dma((2 * groups, 7)), dma((2 * groups, 7))]
        + [dma((15,)), dma((15,))],
        input_output_aliases={6: 0},
        compiler_params=pltpu.CompilerParams(
            collective_id=groups, has_side_effects=True, vmem_limit_bytes=67043328
        ),
        name="wave",
    )(start, table, *vectors, out, toks, *base_weights, *stores)


def shards(
    tokens,
    lengths,
    adapter_ids,
    adapter_place,
    attention_qkv_weight,
    attention_out_weight,
    widen_weight,
    contract_weight,
    first_gain,
    first_shift,
    second_gain,
    second_shift,
    *stores,
):
    i32 = jnp.int32
    col = lax.axis_index("col")
    row = lax.axis_index("row")
    stored = stores[0].shape[0]
    match = adapter_ids[:, None] == jnp.arange(adapter_place.shape[0], dtype=i32)[None, :]
    position = jnp.sum(jnp.where(match, adapter_place[None, :], 0), axis=1)
    meta = jnp.zeros((8, 128), i32)
    meta = meta.at[0, :REQ_COL].set(position).at[1, :REQ_COL].set(lengths)
    tok_all, meta_all = entry_gather(tokens.T, meta)
    tok_all = tok_all.reshape(64, SLOT, 256)

    requests = 64
    position = meta_all[:, 0, :REQ_COL].reshape(requests)
    length = meta_all[:, 1, :REQ_COL].reshape(requests)
    owner, local = position // stored, position % stored
    n = jnp.arange(requests, dtype=i32)
    same = (owner[None, :] == owner[:, None]) & (n[None, :] < n[:, None])
    rank = jnp.sum(same.astype(i32), axis=1)
    near = jnp.sum((same & (n[None, :] // REQ_COL == n[:, None] // REQ_COL)).astype(i32), axis=1)
    waves = (jnp.max(rank) + K) // K
    mine = owner == col
    own_rank = jnp.where(mine, rank, -1)
    source = owner * 2 + near
    keys = [own_rank] * 3 + [jnp.where(mine, n // REQ_COL * 2 + near, -1), n, n]
    facts = [n, local, length - 1, rank, source, rank]
    spots = jnp.arange(64, dtype=i32)[None, :]
    spots = spots + col * jnp.array([[0], [0], [0], [0], [REQ_COL], [REQ_COL]], i32)
    hit = jnp.stack(keys)[:, None, :] == spots[:, :, None]
    table = jnp.sum(jnp.where(hit, jnp.stack(facts)[:, None, :], 0), axis=2)
    table = table + jnp.array([[0], [0], [1], [0], [0], [0]], i32)
    vectors = [v[None, :] for v in (first_gain, first_shift, second_gain, second_shift)]
    base_weights = (attention_qkv_weight, attention_out_weight, widen_weight, contract_weight)

    def wave(w, out):
        start = (w * K).astype(i32)[None]
        return run_wave(K // GRP, start, table, vectors, out, tok_all, base_weights, stores)

    out = lax.fori_loop(0, waves, wave, jnp.zeros((8, 256, TOK), bf16))
    return out.reshape(D, TOK)


def solution(mesh):
    return jax.shard_map(
        shards,
        mesh=mesh,
        in_specs=(
            P("row", "col"),
            P("col"),
            P("col"),
            P(),
            P("col", "row"),
            P("col", "row"),
            P("col", "row"),
            P("col", "row"),
            P("row"),
            P(),
            P(),
            P(),
            P("col", None, "row"),
            P("col", None, None, "row"),
            P("col", None, "row"),
            P("col", None, "row"),
            P("col", None, "row"),
            P("col", None, "row"),
            P("col", None, "row"),
            P("col", None, "row"),
        ),
        out_specs=P(None, "col"),
        check_vma=False,
    )
```
